256 devices in a mesh: src: 2 (over z_hi), gx: 8 (over z_lo, core), gy: 16 (over y, x).
Axes of the slice: x: 4, y: 4, z: 8 (z_hi: 2, z_lo: 4; z = z_hi * 4 + z_lo), core: 2. Of those that a mesh axis runs over, the one named last changes fastest.
Arguments:
- forward_state: float32 [4, 6, 128, 65536], P('src', None, 'gx', 'gy'), may hold values from -6 to 6
- adjoint_state: float32 [4, 6, 128, 65536], P('src', None, 'gx', 'gy'), may hold values from -6 to 6
- permittivity: float32 [128, 65536], P('gx', 'gy'), may hold values from 1 to 3
- waveform: float32 [4, 4], P('src'), may hold values from -8 to 8
- source_cell: int32 [4, 3], P('src'), may hold values from 0 to 1023, as said below
- block_owner: int32 [32, 256], P('gx', 'gy'), may hold values from -1 to 15, as said below
- block_slot: int32 [32, 256], P('gx', 'gy'), may hold values from -1 to 3, as said below
- owner_rows: int32 [128, 64], P(('gx', 'gy')), may hold values from 0 to 63, as said below
Outputs:
- design_gradient: float32 [8192, 1024], P(('gx', 'gy'), 'src')
The draws below stay inside these ranges and needn't reach their ends.
Inputs may be any that keep to these rules, and one draw needn't show every extreme that they name: `block_owner`: -1 marks a block outside the design region; otherwise the owner lies in the block's own gx row. The design blocks of one device that go to one owner number at most 4, and some device sends exactly 4 to some owner. `block_slot`: -1 exactly where block_owner is -1; the blocks that one device sends to one owner have distinct slots. `owner_rows`: each row is a permutation of 0 to 63. `source_cell`: each row is a cell (x, y, z) of the grid.
All inputs are finite; a program needn't handle non-finite values.
Results may differ from the reference program's by a relative error of at most 0.0003.
Values sent between devices are 32-bit elements; how exact they have to be, the bound alone decides.
No kernel may reach another device: no remote copies, remote signals or barrier semaphores. Data moves between devices by JAX's collectives and lax.ppermute only.
A program may use at most 128 MiB of HBM per device.

```python
import math
import jax
import jax.numpy as jnp
from jax import lax

CX = 16
CY = 64
NZ = 64
STEPS = 4
BX = 4
BY = 4
SOURCES = 4
NX = 128
NY = 1024
NYZ = 65536
LBX = 4
LBY = 16
LB = 64
NBX = 32
NBY = 256
CAP = 4
PD = 64
ROWS = 8192
N_GX = 8
N_GY = 16


def chosen_row(key):
    return jax.random.randint(jax.random.fold_in(key, 5), (), 0, N_GX)


def design_layout(key):
    devices = N_GX * N_GY
    base_key = jax.random.fold_in(key, 11)
    raw_counts = jax.random.randint(jax.random.fold_in(base_key, 1), (devices,), 0, LB + 1)
    counts = raw_counts * raw_counts // LB
    device_row = jnp.arange(devices) // N_GY
    counts = jnp.where(device_row == chosen_row(key), LB, counts)
    subkeys = jax.random.split(jax.random.fold_in(base_key, 2), devices)
    orders = jax.vmap(lambda single: jax.random.permutation(single, LB))(subkeys)
    position = jnp.argsort(orders, axis=1)
    offsets = jax.random.randint(jax.random.fold_in(base_key, 3), (devices, 1), 0, N_GY)
    column = (jnp.arange(devices) % N_GY)[:, None]
    design = position < counts[:, None]
    owners = jnp.where(design, (column + offsets + position // CAP) % N_GY, -1)
    slots = jnp.where(design, position % CAP, -1)

    def arrange(values):
        return values.reshape(N_GX, N_GY, LBX, LBY).transpose(0, 2, 1, 3).reshape(NBX, NBY).astype(jnp.int32)
    return (arrange(owners), arrange(slots))


def draw_block_owner(key, part):
    return design_layout(key)[0]


def draw_block_slot(key, part):
    return design_layout(key)[1]


def draw_owner_rows(key, part):
    subkeys = jax.random.split(jax.random.fold_in(key, 17), N_GX * N_GY)
    return jax.vmap(lambda single: jax.random.permutation(single, PD))(subkeys).astype(jnp.int32)


def draw_source_cell(key, part):
    base_key = jax.random.fold_in(key, 23)
    picked = jax.random.randint(jax.random.fold_in(base_key, 1), (SOURCES,), 0, N_GY)
    cell_x = chosen_row(key) * CX + jax.random.randint(jax.random.fold_in(base_key, 2), (SOURCES,), 0, CX)
    cell_y = picked * CY + jax.random.randint(jax.random.fold_in(base_key, 3), (SOURCES,), 0, CY)
    cell_z = jax.random.randint(jax.random.fold_in(base_key, 4), (SOURCES,), 0, NZ)
    first = jnp.arange(SOURCES) == 0
    if NY >= NX and NY >= NZ:
        cell_y = jnp.where(first, NY - 1, cell_y)
        cell_z = jnp.where(first, 0, cell_z)
    elif NX >= NZ:
        cell_x = jnp.where(first, NX - 1, cell_x)
        cell_z = jnp.where(first, 0, cell_z)
    else:
        cell_z = jnp.where(first, NZ - 1, cell_z)
        cell_y = jnp.where(first, 0, cell_y)
    return jnp.stack([cell_x, cell_y, cell_z], axis=1).astype(jnp.int32)


def shard_levels(own_key, extent, cuts, smallest, high):
    loudness = 1.0
    for dim, shards_of in cuts:
        heights = jax.random.uniform(jax.random.fold_in(jax.random.fold_in(own_key, 6), dim), (shards_of,), jnp.float32, smallest / len(cuts), high / len(cuts))
        loudness = loudness * jnp.repeat(jnp.exp(heights), extent[dim] // shards_of).reshape((-1,) + (1,) * (len(extent) - 1 - dim))
    return loudness


def centred(own_key, extent, spread, bound, cuts=(), dtype=jnp.bfloat16):
    array = spread * jax.random.normal(own_key, extent, jnp.float32)
    if cuts:
        array = array * shard_levels(own_key, extent, cuts, -0.22, 0.18)
    return jnp.clip(array, -bound, bound).astype(dtype)


def setup_inputs(seed: int = 0) -> dict:
    key_of = jax.random.split(jax.random.key(seed), 9)
    return {
        "forward_state": centred(key_of[0], (SOURCES, 6, NX, NYZ), 1.0, 6.0, ((0, 2), (2, 8), (3, 16)), jnp.float32),
        "adjoint_state": centred(key_of[1], (SOURCES, 6, NX, NYZ), 1.0, 6.0, ((0, 2), (2, 8), (3, 16)), jnp.float32),
        "permittivity": jnp.clip(jnp.exp(math.log(3.0) - 1.0986123 * jax.random.uniform(key_of[2], (NX, NYZ), jnp.float32) ** shard_levels(key_of[2], (NX, NYZ), ((0, 8), (1, 16)), -0.2, 0.2)), 1.0, 3.0),
        "waveform": centred(key_of[3], (SOURCES, STEPS), 2.0, 8.0, ((0, 2),), jnp.float32),
        "source_cell": draw_source_cell(jax.random.fold_in(key_of[8], 71), 0),
        "block_owner": draw_block_owner(jax.random.fold_in(key_of[8], 71), 0),
        "block_slot": draw_block_slot(jax.random.fold_in(key_of[8], 71), 0),
        "owner_rows": draw_owner_rows(jax.random.fold_in(key_of[8], 71), 0),
    }


courant = 0.55


def upper_z(values, z_cells):
    zindex = lax.broadcasted_iota(jnp.int32, values.shape, values.ndim - 1) % z_cells
    shifted = jnp.concatenate([values[..., 1:], jnp.zeros_like(values[..., :1])], axis=-1)
    return jnp.where(zindex == z_cells - 1, jnp.zeros_like(shifted), shifted)


def lower_z(values, z_cells):
    zindex = lax.broadcasted_iota(jnp.int32, values.shape, values.ndim - 1) % z_cells
    shifted = jnp.concatenate([jnp.zeros_like(values[..., :1]), values[..., :-1]], axis=-1)
    return jnp.where(zindex == 0, jnp.zeros_like(shifted), shifted)


def upper_x(values, ghosts):
    return jnp.concatenate([values[..., 1:, :], ghosts], axis=-2)


def lower_x(values, ghosts):
    return jnp.concatenate([ghosts, values[..., :-1, :]], axis=-2)


def upper_y(values, ghosts, z_cells):
    return jnp.concatenate([values[..., z_cells:], ghosts], axis=-1)


def lower_y(values, ghosts, z_cells):
    return jnp.concatenate([ghosts, values[..., :-z_cells]], axis=-1)


def magnetic_update(electric, magnetic, ghost_x, ghost_y, z_cells):
    new_hx = magnetic[0] - courant * ((upper_y(electric[2], ghost_y[1], z_cells) - electric[2]) - (upper_z(electric[1], z_cells) - electric[1]))
    new_hy = magnetic[1] - courant * ((upper_z(electric[0], z_cells) - electric[0]) - (upper_x(electric[2], ghost_x[1]) - electric[2]))
    new_hz = magnetic[2] - courant * ((upper_x(electric[1], ghost_x[0]) - electric[1]) - (upper_y(electric[0], ghost_y[0], z_cells) - electric[0]))
    return (new_hx, new_hy, new_hz)


def electric_update(electric, magnetic, ghost_x, ghost_y, factor, z_cells):
    new_ex = electric[0] + factor * ((magnetic[2] - lower_y(magnetic[2], ghost_y[1], z_cells)) - (magnetic[1] - lower_z(magnetic[1], z_cells)))
    new_ey = electric[1] + factor * ((magnetic[0] - lower_z(magnetic[0], z_cells)) - (magnetic[2] - lower_x(magnetic[2], ghost_x[1])))
    new_ez = electric[2] + factor * ((magnetic[1] - lower_x(magnetic[1], ghost_x[0])) - (magnetic[0] - lower_y(magnetic[0], ghost_y[0], z_cells)))
    return (new_ex, new_ey, new_ez)


def reference(forward_state, adjoint_state, permittivity, waveform, source_cell, block_owner, block_slot, owner_rows):
    factor = courant / permittivity
    cells_x, cells_yz = permittivity.shape
    x_index = lax.broadcasted_iota(jnp.int32, (cells_x, cells_yz), 0)
    yz_index = lax.broadcasted_iota(jnp.int32, (cells_x, cells_yz), 1)
    empty_x = jnp.zeros((1, cells_yz), jnp.float32)
    empty_y = jnp.zeros((cells_x, NZ), jnp.float32)
    ghost_x = (empty_x, empty_x)
    ghost_y = (empty_y, empty_y)

    def advance(electric, magnetic):
        magnetic = magnetic_update(electric, magnetic, ghost_x, ghost_y, NZ)
        electric = electric_update(electric, magnetic, ghost_x, ghost_y, factor, NZ)
        return electric, magnetic

    def one_source(running, inputs):
        forward, adjoint, pulses, location = inputs
        beacon = ((x_index == location[0]) & (yz_index == location[1] * NZ + location[2])).astype(jnp.float32)
        electric = (forward[0], forward[1], forward[2])
        magnetic = (forward[3], forward[4], forward[5])
        increments = []
        for step_index in range(STEPS):
            updated, magnetic = advance(electric, magnetic)
            updated = (updated[0], updated[1], updated[2] + pulses[step_index] * beacon)
            increments.append((updated[0] - electric[0], updated[1] - electric[1], updated[2] - electric[2]))
            electric = updated
        electric = (adjoint[0], adjoint[1], adjoint[2])
        magnetic = (adjoint[3], adjoint[4], adjoint[5])
        density = jnp.zeros((cells_x, cells_yz), jnp.float32)
        for step_index in range(STEPS):
            electric, magnetic = advance(electric, magnetic)
            paired = increments[STEPS - 1 - step_index]
            density = density + (electric[0] * paired[0] + electric[1] * paired[1] + electric[2] * paired[2])
        return running + density, None

    summed, _ = lax.scan(one_source, jnp.zeros((cells_x, cells_yz), jnp.float32), (forward_state, adjoint_state, waveform, source_cell))
    gradient = -summed / permittivity
    blocks = gradient.reshape(NBX, BX, NBY, BY, NZ).transpose(0, 2, 1, 3, 4).reshape(NBX, NBY, BX * BY * NZ)
    row_group = lax.broadcasted_iota(jnp.int32, (NBX, NBY), 0) // LBX
    sender = lax.broadcasted_iota(jnp.int32, (NBX, NBY), 1) // LBY
    owner_safe = jnp.maximum(block_owner, 0)
    slot_safe = jnp.maximum(block_slot, 0)
    owner_device = row_group * N_GY + owner_safe
    target = owner_device * PD + owner_rows[owner_device, sender * CAP + slot_safe]
    target = jnp.where(block_owner >= 0, target, ROWS).astype(jnp.int32)
    placed = jnp.zeros((ROWS, BX * BY * NZ), jnp.float32)
    return placed.at[target.reshape(-1)].set(blocks.reshape(-1, BX * BY * NZ), mode="drop")
```

```python
import functools

import jax
import jax.numpy as jnp
from jax import lax
from jax.experimental import pallas as pl
from jax.experimental.pallas import tpu as pltpu
from jax.sharding import PartitionSpec as P

NZ = 64
STEPS = 4
BX = 4
BY = 4
HALO = 4
CX = 16
XR = CX + 2 * HALO
TJ = 32
TE = TJ + 4
ROWS = (TE + 2) * XR
W = 128
COURANT = 0.55
F32 = jnp.float32


def shifted_pairs(count, by):
    return [(i, i + by) for i in range(count) if 0 <= i + by < count]


def passed_along(shard, axis, by):
    return lax.ppermute(shard, axis, shifted_pairs(lax.axis_size(axis), by))


def lanes(tile):
    return pl.ds(tile * W, W)


def pack_first(adj, fwd_lo, fwd_hi, eps_lo, eps_hi, ax_up, ax_dn, fy_up, fy_dn):
    def one(k, _):
        s, c = k // 6, k % 6
        for j in range(TJ):
            row = pl.multiple_of((k * TJ + j) * 4, 4)
            ax_dn[pl.ds(row, 4), :] = adj[s, c, 0:4, lanes(j)]
            ax_up[pl.ds(row, 4), :] = adj[s, c, CX - 4 : CX, lanes(j)]
        for j in range(2):
            row = pl.multiple_of((k * 2 + j) * CX, CX)
            fy_dn[pl.ds(row, CX), :] = fwd_lo[s, c, :, lanes(j)]
            fy_up[pl.ds(row, CX), :] = fwd_hi[s, c, :, lanes(j)]
        return 0

    lax.fori_loop(0, 12, one, 0)
    for j in range(2):
        row = (12 * 2 + j) * CX
        fy_dn[pl.ds(row, CX), :] = COURANT / eps_lo[:, lanes(j)]
        fy_up[pl.ds(row, CX), :] = COURANT / eps_hi[:, lanes(j)]


def pack_forward_x(fwd, eps, fy_lo, fy_hi, fx_up, fx_dn):
    def ghosts(k):
        for j in range(2):
            src = pl.multiple_of((k * 2 + j) * CX, CX)
            lo = pl.multiple_of((k * TE + j) * 4, 4)
            hi = pl.multiple_of((k * TE + TJ + 2 + j) * 4, 4)
            fx_dn[pl.ds(lo, 4), :] = fy_lo[pl.ds(src, 4), :]
            fx_up[pl.ds(lo, 4), :] = fy_lo[pl.ds(src + CX - 4, 4), :]
            fx_dn[pl.ds(hi, 4), :] = fy_hi[pl.ds(src, 4), :]
            fx_up[pl.ds(hi, 4), :] = fy_hi[pl.ds(src + CX - 4, 4), :]

    def one(k, _):
        s, c = k // 6, k % 6
        for j in range(TJ):
            row = pl.multiple_of((k * TE + 2 + j) * 4, 4)
            fx_dn[pl.ds(row, 4), :] = fwd[s, c, 0:4, lanes(j)]
            fx_up[pl.ds(row, 4), :] = fwd[s, c, CX - 4 : CX, lanes(j)]
        ghosts(k)
        return 0

    lax.fori_loop(0, 12, one, 0)
    for j in range(TJ):
        row = (12 * TE + 2 + j) * 4
        fx_dn[pl.ds(row, 4), :] = COURANT / eps[0:4, lanes(j)]
        fx_up[pl.ds(row, 4), :] = COURANT / eps[CX - 4 : CX, lanes(j)]
    ghosts(12)


def pack_adjoint_y(adj_lo, adj_hi, ax_lo, ax_hi, ay_up, ay_dn):
    def one(k, _):
        s, c = k // 6, k % 6
        for j in range(2):
            base = pl.multiple_of((k * 2 + j) * XR, 8)
            for out, own, tile in ((ay_dn, adj_lo, j), (ay_up, adj_hi, TJ - 2 + j)):
                src = pl.multiple_of((k * TJ + tile) * 4, 4)
                out[pl.ds(base, 4), :] = ax_lo[pl.ds(src, 4), :]
                out[pl.ds(base + 4, CX), :] = own[s, c, :, lanes(j)]
                out[pl.ds(base + 4 + CX, 4), :] = ax_hi[pl.ds(src, 4), :]
        return 0

    lax.fori_loop(0, 12, one, 0)


def simulate(
    where,
    owners,
    slots,
    cells,
    wave,
    fwd,
    adj,
    eps,
    fy_lo,
    fy_hi,
    fx_lo,
    fx_hi,
    ax_lo,
    ax_hi,
    ay_lo,
    ay_hi,
    out,
    field,
    factor,
    inc,
    density,
    block,
):
    at_x0, at_x1, at_y0, at_y1, gx, gy = (where[i] for i in range(6))
    lane = lax.broadcasted_iota(jnp.int32, (8, W), 1)
    row8 = lax.broadcasted_iota(jnp.int32, (8, W), 0)
    low = lane < NZ
    z_first = (lane & (NZ - 1)) == 0
    z_last = (lane & (NZ - 1)) == NZ - 1
    coef_x = [
        jnp.where((row8 < 4) & (at_x0 == 1), 0.0, COURANT).astype(F32),
        jnp.full((8, W), COURANT, F32),
        jnp.where((row8 >= 4) & (at_x1 == 1), 0.0, COURANT).astype(F32),
    ]

    zeros = jnp.zeros((XR, W), F32)
    for k in range(12):
        field[k, pl.ds(0, XR), :] = zeros
        field[k, pl.ds((TE + 1) * XR, XR), :] = zeros
    factor[pl.ds(0, XR), :] = zeros
    factor[pl.ds((TE + 1) * XR, XR), :] = zeros

    def fill_forward(put, k, own):
        for j in range(TJ):
            r = (j + 3) * XR
            put(r + 4, own(j))
            src = pl.multiple_of((k * TE + 2 + j) * 4, 4)
            put(r, fx_lo[pl.ds(src, 4), :])
            put(r + 4 + CX, fx_hi[pl.ds(src, 4), :])
        for j, ghost, g in ((0, fy_lo, 0), (1, fy_lo, 1), (TE - 2, fy_hi, 0), (TE - 1, fy_hi, 1)):
            r = (j + 1) * XR
            src = pl.multiple_of((k * 2 + g) * CX, CX)
            put(r + 4, ghost[pl.ds(src, CX), :])
            src = pl.multiple_of((k * TE + j) * 4, 4)
            put(r, fx_lo[pl.ds(src, 4), :])
            put(r + 4 + CX, fx_hi[pl.ds(src, 4), :])

    def load_forward(k, _):
        def put(r, v):
            field[k, pl.ds(r, v.shape[0]), :] = v

        fill_forward(put, k, lambda j: fwd[k // 6, k % 6, :, lanes(j)])
        return 0

    def load_adjoint(k, _):
        def put(r, v):
            field[k, pl.ds(r, v.shape[0]), :] = v

        for j in range(TJ):
            r = (j + 3) * XR
            put(r + 4, adj[k // 6, k % 6, :, lanes(j)])
            src = pl.multiple_of((k * TJ + j) * 4, 4)
            put(r, ax_lo[pl.ds(src, 4), :])
            put(r + 4 + CX, ax_hi[pl.ds(src, 4), :])
        for j, ghost, g in ((0, ay_lo, 0), (1, ay_lo, 1), (TE - 2, ay_hi, 0), (TE - 1, ay_hi, 1)):
            src = pl.multiple_of((k * 2 + g) * XR, 8)
            put((j + 1) * XR, ghost[pl.ds(src, XR), :])
        return 0

    def up_z(v):
        return jnp.where(z_last, 0.0, pltpu.roll(v, W - 1, 1))

    def down_z(v):
        return jnp.where(z_first, 0.0, pltpu.roll(v, 1, 1))

    def up_y(v, after):
        return pltpu.roll(jnp.where(low, after, v), NZ, 1)

    def down_y(v, before):
        return pltpu.roll(jnp.where(low, v, before), NZ, 1)

    def magnetic(j, _):
        inside = jnp.where(
            ((j < 2) & (at_y0 == 1)) | ((j >= TE - 2) & (at_y1 == 1)), 0.0, 1.0
        ).astype(F32)
        done = []
        for t in range(3):
            b = pl.multiple_of((j + 1) * XR + 8 * t, 8)
            c = coef_x[t] * inside
            for s in range(2):
                k = 6 * s
                ex = field[k, pl.ds(b, 8), :]
                ey = field[k + 1, pl.ds(b, 8), :]
                ez = field[k + 2, pl.ds(b, 8), :]
                ex_y = up_y(ex, field[k, pl.ds(b + XR, 8), :])
                ez_y = up_y(ez, field[k + 2, pl.ds(b + XR, 8), :])
                ey_x = field[k + 1, pl.ds(b + 1, 8), :]
                ez_x = field[k + 2, pl.ds(b + 1, 8), :]
                hx = field[k + 3, pl.ds(b, 8), :]
                hy = field[k + 4, pl.ds(b, 8), :]
                hz = field[k + 5, pl.ds(b, 8), :]
                hx = hx - c * ((ez_y - ez) - (up_z(ey) - ey))
                hy = hy - c * ((up_z(ex) - ex) - (ez_x - ez))
                hz = hz - c * ((ey_x - ey) - (ex_y - ex))
                done.append((k, b, hx, hy, hz))
        for k, b, hx, hy, hz in done:
            field[k + 3, pl.ds(b, 8), :] = hx
            field[k + 4, pl.ds(b, 8), :] = hy
            field[k + 5, pl.ds(b, 8), :] = hz
        return 0

    def electric(j, step, adjoint):
        done = []
        for t in range(3):
            b = pl.multiple_of((j + 1) * XR + 8 * t, 8)
            a = pl.multiple_of(j * XR + 8 * t, 8)
            f = factor[pl.ds(b, 8), :]
            total = density[pl.ds(a, 8), :] if adjoint else None
            for s in range(2):
                k = 6 * s
                hx = field[k + 3, pl.ds(b, 8), :]
                hy = field[k + 4, pl.ds(b, 8), :]
                hz = field[k + 5, pl.ds(b, 8), :]
                hx_y = down_y(hx, field[k + 3, pl.ds(b - XR, 8), :])
                hz_y = down_y(hz, field[k + 5, pl.ds(b - XR, 8), :])
                hy_x = field[k + 4, pl.ds(b - 1, 8), :]
                hz_x = field[k + 5, pl.ds(b - 1, 8), :]
                ex = field[k, pl.ds(b, 8), :]
                ey = field[k + 1, pl.ds(b, 8), :]
                ez = field[k + 2, pl.ds(b, 8), :]
                nx = ex + f * ((hz - hz_y) - (hy - down_z(hy)))
                ny = ey + f * ((hx - down_z(hx)) - (hz - hz_x))
                nz = ez + f * ((hy - hy_x) - (hx - hx_y))
                i = 3 * s
                if adjoint:
                    total = total + (
                        nx * inc[step, i, pl.ds(a, 8), :]
                        + ny * inc[step, i + 1, pl.ds(a, 8), :]
                        + nz * inc[step, i + 2, pl.ds(a, 8), :]
                    )
                    done.append((k, i, a, b, nx, ny, nz, None))
                else:
                    done.append((k, i, a, b, nx, ny, nz, (nx - ex, ny - ey, nz - ez)))
            if adjoint:
                done.append((None, None, a, None, total, None, None, None))
        for k, i, a, b, nx, ny, nz, grown in done:
            if k is None:
                density[pl.ds(a, 8), :] = nx
                continue
            field[k, pl.ds(b, 8), :] = nx
            field[k + 1, pl.ds(b, 8), :] = ny
            field[k + 2, pl.ds(b, 8), :] = nz
            if grown is not None:
                for m in range(3):
                    inc[step, i + m, pl.ds(a, 8), :] = grown[m]
        return 0

    spans_h = ((0, TE), (0, TE - 1), (1, TE - 1), (1, TE - 2))
    spans_e = ((0, TE), (1, TE - 1), (1, TE - 1), (2, TE - 2))

    lax.fori_loop(0, 12, load_forward, 0)

    def put_factor(r, v):
        factor[pl.ds(r, v.shape[0]), :] = v

    fill_forward(put_factor, 12, lambda j: COURANT / eps[:, lanes(j)])

    for n in range(STEPS):
        lax.fori_loop(*spans_h[n], magnetic, 0)
        lax.fori_loop(*spans_e[n], lambda j, _: electric(j, n, False), 0)
        for s in range(2):
            x = cells[s, 0] - gx * CX + HALO
            y = cells[s, 1] - gy * (2 * TJ) + HALO
            z = cells[s, 2]

            @pl.when((x >= 0) & (x < XR) & (y >= 0) & (y < 2 * TE))
            def _():
                r = (y // 2) * XR + x
                here = lax.broadcasted_iota(jnp.int32, (1, W), 1) == (y % 2) * NZ + z
                pulse = jnp.where(here, wave[s, n], 0.0).astype(F32)
                field[6 * s + 2, pl.ds(r + XR, 1), :] += pulse
                inc[n, 3 * s + 2, pl.ds(r, 1), :] += pulse

    lax.fori_loop(0, 12, load_adjoint, 0)
    density[...] = jnp.zeros_like(density)
    for n in range(STEPS):
        lax.fori_loop(*spans_h[n], magnetic, 0)
        lax.fori_loop(*spans_e[n], lambda j, _: electric(j, STEPS - 1 - n, True), 0)

    for j in range(TJ):
        for t in range(2):
            g = density[pl.ds((j + 2) * XR + 4 + 8 * t, 8), :]
            g = -g / eps[8 * t : 8 * t + 8, lanes(j)]
            for h in range(2):
                b = ((2 * t + h) * (TJ // 2) + j // 2) * 8 + j % 2
                block[pl.ds(b, 4, stride=2), :] = g[4 * h : 4 * h + 4]
    out[...] = jnp.zeros_like(out)

    def send(i, _):
        o = owners[i]

        @pl.when(o >= 0)
        def _():
            c = pl.multiple_of(slots[i] * 4, 4)
            b = pl.multiple_of(i * 8, 8)
            out[o, pl.ds(c, 4), :] = block[pl.ds(b, 4), :]
            out[16 + o, pl.ds(c, 4), :] = block[pl.ds(b + 4, 4), :]

        return 0

    lax.fori_loop(0, 64, send, 0)


def place(rows, arrived, out, wide):
    def one(g, _):
        v = arrived[g] + arrived[16 + g]
        for c in range(4):
            r = pl.multiple_of(rows[g * 4 + c] * 4, 4)
            wide[pl.ds(r, 4), :] = v[c * 4 : c * 4 + 4]
        return 0

    lax.fori_loop(0, 16, one, 0)
    for i in range(8):
        for q in range(4):
            out[8 * i : 8 * i + 8, lanes(q)] = wide[pl.ds(32 * i + q, 8, stride=4), :]


def per_device(
    forward_state,
    adjoint_state,
    permittivity,
    waveform,
    source_cell,
    block_owner,
    block_slot,
    owner_rows,
):
    full = pl.BlockSpec(memory_space=pltpu.VMEM)
    scalars = pl.BlockSpec(memory_space=pltpu.SMEM)
    params = functools.partial(pltpu.CompilerParams)

    def buf(*shape):
        return jax.ShapeDtypeStruct(shape, F32)

    strip = (2, 6, CX, 2 * W)
    s_lo = pl.BlockSpec(strip, lambda i: (0, 0, 0, 0))
    s_hi = pl.BlockSpec(strip, lambda i: (0, 0, 0, TJ // 2 - 1))
    e_lo = pl.BlockSpec((CX, 2 * W), lambda i: (0, 0))
    e_hi = pl.BlockSpec((CX, 2 * W), lambda i: (0, TJ // 2 - 1))
    state = pl.BlockSpec((2, 6, CX, TJ * W), lambda i: (0, 0, 0, 0))
    whole = lambda *shape: pl.BlockSpec(shape, lambda i: (0,) * len(shape))

    ax_n, fy_n, fx_n, ay_n = 12 * TJ * 4, 13 * 2 * CX, 13 * TE * 4, 12 * 2 * XR
    ax_up, ax_dn, fy_up, fy_dn = pl.pallas_call(
        pack_first,
        grid=(1,),
        in_specs=[state, s_lo, s_hi, e_lo, e_hi],
        out_specs=[whole(ax_n, W)] * 2 + [whole(fy_n, W)] * 2,
        out_shape=[buf(ax_n, W)] * 2 + [buf(fy_n, W)] * 2,
        compiler_params=params(vmem_limit_bytes=24 << 20),
        name="pack_first",
    )(adjoint_state, forward_state, forward_state, permittivity, permittivity)

    ax_lo = passed_along(ax_up, "gx", 1)
    ax_hi = passed_along(ax_dn, "gx", -1)
    fy_lo = passed_along(fy_up, "gy", 1)
    fy_hi = passed_along(fy_dn, "gy", -1)

    fx_up, fx_dn = pl.pallas_call(
        pack_forward_x,
        in_specs=[full] * 4,
        out_specs=[full] * 2,
        out_shape=[buf(fx_n, W)] * 2,
        compiler_params=params(vmem_limit_bytes=24 << 20),
        name="pack_forward_x",
    )(forward_state, permittivity, fy_lo, fy_hi)
    fx_lo = passed_along(fx_up, "gx", 1)
    fx_hi = passed_along(fx_dn, "gx", -1)

    ay_up, ay_dn = pl.pallas_call(
        pack_adjoint_y,
        grid=(1,),
        in_specs=[s_lo, s_hi, whole(ax_n, W), whole(ax_n, W)],
        out_specs=[whole(ay_n, W)] * 2,
        out_shape=[buf(ay_n, W)] * 2,
        compiler_params=params(vmem_limit_bytes=24 << 20),
        name="pack_adjoint_y",
    )(adjoint_state, adjoint_state, ax_lo, ax_hi)
    ay_lo = passed_along(ay_up, "gy", 1)
    ay_hi = passed_along(ay_dn, "gy", -1)

    gx, gy = lax.axis_index("gx"), lax.axis_index("gy")
    where = jnp.stack(
        [
            gx == 0,
            gx == lax.axis_size("gx") - 1,
            gy == 0,
            gy == lax.axis_size("gy") - 1,
            gx,
            gy,
        ]
    ).astype(jnp.int32)
    outgoing = pl.pallas_call(
        simulate,
        in_specs=[scalars] * 5 + [full] * 11,
        out_specs=full,
        out_shape=buf(32, 16, W),
        scratch_shapes=[
            pltpu.VMEM((12, ROWS, W), F32),
            pltpu.VMEM((ROWS, W), F32),
            pltpu.VMEM((STEPS, 6, TE * XR, W), F32),
            pltpu.VMEM((TE * XR, W), F32),
            pltpu.VMEM((64 * 8, W), F32),
        ],
        compiler_params=params(vmem_limit_bytes=56 << 20),
        name="simulate",
    )(
        where,
        block_owner.reshape(-1),
        block_slot.reshape(-1),
        source_cell,
        waveform,
        forward_state,
        adjoint_state,
        permittivity,
        fy_lo,
        fy_hi,
        fx_lo,
        fx_hi,
        ax_lo,
        ax_hi,
        ay_lo,
        ay_hi,
    )
    arrived = lax.all_to_all(outgoing, ("src", "gy"), 0, 0, tiled=True)
    return pl.pallas_call(
        place,
        in_specs=[scalars, full],
        out_specs=full,
        out_shape=buf(64, 512),
        scratch_shapes=[pltpu.VMEM((256, W), F32)],
        name="place",
    )(owner_rows.reshape(-1), arrived)


def solution(mesh):
    in_specs = (
        P("src", None, "gx", "gy"),
        P("src", None, "gx", "gy"),
        P("gx", "gy"),
        P("src", None),
        P("src", None),
        P("gx", "gy"),
        P("gx", "gy"),
        P(("gx", "gy"), None),
    )
    out_specs = P(("gx", "gy"), "src")
    return jax.shard_map(
        per_device, mesh=mesh, in_specs=in_specs, out_specs=out_specs, check_vma=False
    )
```

```python
import jax
import jax.numpy as jnp
from jax import lax
from jax.experimental import pallas as pl
from jax.experimental.pallas import tpu as pltpu
from jax.sharding import PartitionSpec as P

NZ = 64
STEPS = 4
HALO = 4
CX = 16
XR = CX + 2 * HALO
CY = 64
TJ = CY // 2
HY = CY // 2
TR = HY + 2 * HALO
ROWS = TR * XR
UNROLL = 4
W = 128
COURANT = 0.55
F32 = jnp.float32


def passed_along(shard, axis, by):
    count = lax.axis_size(axis)
    pairs = [(i, i + by) for i in range(count) if 0 <= i + by < count]
    return lax.ppermute(shard, axis, pairs)


def lanes(tile):
    return pl.ds(tile * W, W)


def aligned(index, step):
    return index if isinstance(index, int) else pl.multiple_of(index, step)


def pack_x(state, *rest):
    eps, up, dn = rest if len(rest) == 3 else (None, *rest)

    def put(k, get):
        for j in range(TJ):
            row = aligned((k * TJ + j) * 4, 4)
            dn[pl.ds(row, 4), :] = get(pl.ds(0, 4), lanes(j))
            up[pl.ds(row, 4), :] = get(pl.ds(CX - 4, 4), lanes(j))

    def one(k, _):
        put(k, lambda x, j: state[k // 6, k % 6, x, j])
        return 0

    lax.fori_loop(0, 12, one, 0)
    if eps is not None:
        put(12, lambda x, j: COURANT / eps[x, j])


def pack_y(own_lo, own_hi, *rest):
    eps = None
    if len(rest) == 6:
        eps, rest = rest[:2], rest[2:]
    x_lo, x_hi, up, dn = rest

    def put(k, get):
        for j in range(2):
            base = aligned((k * 2 + j) * XR, 8)
            for out, side, tile in ((dn, 0, j), (up, 1, TJ - 2 + j)):
                row = aligned((k * TJ + tile) * 4, 4)
                out[pl.ds(base, 4), :] = x_lo[pl.ds(row, 4), :]
                out[pl.ds(base + 4, CX), :] = get(side, lanes(j))
                out[pl.ds(base + 4 + CX, 4), :] = x_hi[pl.ds(row, 4), :]

    def one(k, _):
        put(k, lambda side, j: (own_lo, own_hi)[side][k // 6, k % 6, :, j])
        return 0

    lax.fori_loop(0, 12, one, 0)
    if eps is not None:
        put(12, lambda side, j: COURANT / eps[side][:, j])


def place_field(put, own, k, x_lo, x_hi, y_lo, y_hi, low):
    pieces = ((0, 4), (4, 8), (12, 8), (20, 4))

    def source(j, x, n):
        if j < 0 or j >= TJ:
            ghost, g = (y_lo, j + 2) if j < 0 else (y_hi, j - TJ)
            return ghost[pl.ds(aligned((k * 2 + g) * XR, 8) + x, n), :]
        if n == 8:
            return own(x - 4, j)
        return (x_lo if x == 0 else x_hi)[pl.ds(aligned((k * TJ + j) * 4, 4), 4), :]

    for u in range(TR // 2):
        for x, n in pieces:
            a = source(u - 2, x, n)
            b = source(u - 2 + TJ // 2, x, n)
            first = low[:n]
            put(2 * u * XR + x, jnp.where(first, a, pltpu.roll(b, NZ, 1)))
            put((2 * u + 1) * XR + x, jnp.where(first, pltpu.roll(a, NZ, 1), b))


def masks():
    lane = lax.broadcasted_iota(jnp.int32, (8, W), 1)
    return lane < NZ, (lane & (NZ - 1)) == 0, (lane & (NZ - 1)) == NZ - 1


def half_steps(where, fe, fh, factor):
    low, z_first, z_last = masks()
    row8 = lax.broadcasted_iota(jnp.int32, (8, W), 0)
    at_x0, at_x1, at_y0, at_y1 = (where[i] for i in range(4))
    coef_x = [
        jnp.where((row8 < 4) & (at_x0 == 1), 0.0, COURANT).astype(F32),
        jnp.full((8, W), COURANT, F32),
        jnp.where((row8 >= 4) & (at_x1 == 1), 0.0, COURANT).astype(F32),
    ]

    def up_z(v):
        return jnp.where(z_last, 0.0, pltpu.roll(v, W - 1, 1))

    def down_z(v):
        return jnp.where(z_first, 0.0, pltpu.roll(v, 1, 1))

    def magnetic(r):
        in_low = jnp.where((r < HALO) & (at_y0 == 1), 0.0, 1.0).astype(F32)
        in_high = jnp.where((r >= HALO + HY) & (at_y1 == 1), 0.0, 1.0).astype(F32)
        inside = jnp.where(low, in_low, in_high)
        for t in range(3):
            b = pl.multiple_of(r * XR + 8 * t, 8)
            c = coef_x[t] * inside
            for s in range(2):
                k = 3 * s
                ex = fe[k, pl.ds(b, 8), :]
                ey = fe[k + 1, pl.ds(b, 8), :]
                ez = fe[k + 2, pl.ds(b, 8), :]
                ex_y = fe[k, pl.ds(b + XR, 8), :]
                ez_y = fe[k + 2, pl.ds(b + XR, 8), :]
                ey_x = fe[k + 1, pl.ds(b + 1, 8), :]
                ez_x = fe[k + 2, pl.ds(b + 1, 8), :]
                hx = fh[k, pl.ds(b, 8), :] - c * ((ez_y - ez) - (up_z(ey) - ey))
                hy = fh[k + 1, pl.ds(b, 8), :] - c * ((up_z(ex) - ex) - (ez_x - ez))
                hz = fh[k + 2, pl.ds(b, 8), :] - c * ((ey_x - ey) - (ex_y - ex))
                fh[k, pl.ds(b, 8), :] = hx
                fh[k + 1, pl.ds(b, 8), :] = hy
                fh[k + 2, pl.ds(b, 8), :] = hz

    def electric(r, use):
        for t in range(3):
            b = pl.multiple_of(r * XR + 8 * t, 8)
            f = factor[pl.ds(b, 8), :]
            olds, news = [], []
            for s in range(2):
                k = 3 * s
                hx = fh[k, pl.ds(b, 8), :]
                hy = fh[k + 1, pl.ds(b, 8), :]
                hz = fh[k + 2, pl.ds(b, 8), :]
                hx_y = fh[k, pl.ds(b - XR, 8), :]
                hz_y = fh[k + 2, pl.ds(b - XR, 8), :]
                hy_x = fh[k + 1, pl.ds(b - 1, 8), :]
                hz_x = fh[k + 2, pl.ds(b - 1, 8), :]
                ex, ey, ez = (fe[k + c, pl.ds(b, 8), :] for c in range(3))
                nx = ex + f * ((hz - hz_y) - (hy - down_z(hy)))
                ny = ey + f * ((hx - down_z(hx)) - (hz - hz_x))
                nz = ez + f * ((hy - hy_x) - (hx - hx_y))
                fe[k, pl.ds(b, 8), :] = nx
                fe[k + 1, pl.ds(b, 8), :] = ny
                fe[k + 2, pl.ds(b, 8), :] = nz
                olds += [ex, ey, ez]
                news += [nx, ny, nz]
            use(b, olds, news)

    def over(first, last, one):
        def body(r, _):
            one(r)
            return 0

        lax.fori_loop(first, last, body, 0, unroll=UNROLL)

    def step(n, use):
        over(n, TR - 1 - n, magnetic)
        over(n + 1, TR - 1 - n, lambda r: electric(r, use))

    return step


def forward(
    where, cells, wave, state, eps, x_lo, x_hi, y_lo, y_hi, inc, factor, fe, fh
):
    low = masks()[0]

    def load(k, _):
        for ref, c in ((fe, 0), (fh, 3)):
            q = 6 * (k // 3) + k % 3 + c

            def put(r, v):
                ref[k, pl.ds(r, v.shape[0]), :] = v

            own = lambda x, j: state[k // 3, k % 3 + c, pl.ds(x, 8), lanes(j)]
            place_field(put, own, q, x_lo, x_hi, y_lo, y_hi, low)
        return 0

    lax.fori_loop(0, 6, load, 0)

    def put(r, v):
        factor[pl.ds(r, v.shape[0]), :] = v

    place_field(
        put, lambda x, j: COURANT / eps[pl.ds(x, 8), lanes(j)], 12, x_lo, x_hi, y_lo, y_hi, low
    )
    step = half_steps(where, fe, fh, factor)
    lane = lax.broadcasted_iota(jnp.int32, (1, W), 1)
    for n in range(STEPS):

        def use(b, olds, news):
            for i in range(6):
                inc[n, i, pl.ds(b, 8), :] = news[i] - olds[i]

        step(n, use)
        for s in range(2):
            x = cells[s, 0] - where[4] * CX + HALO
            y = cells[s, 1] - where[5] * CY + HALO
            for h in range(2):
                r = y - h * HY

                @pl.when((x >= 0) & (x < XR) & (r >= 0) & (r < TR))
                def _():
                    at = pl.ds(r * XR + x, 1)
                    pulse = jnp.where(lane == h * NZ + cells[s, 2], wave[s, n], 0.0).astype(F32)
                    fe[3 * s + 2, at, :] += pulse
                    inc[n, 3 * s + 2, at, :] += pulse


def adjoint(
    where, owners, slots, state, factor, inc, x_lo, x_hi, y_lo, y_hi, out, fe, fh, density, block
):
    low = masks()[0]

    def load(k, _):
        for ref, c in ((fe, 0), (fh, 3)):
            q = 6 * (k // 3) + k % 3 + c

            def put(r, v):
                ref[k, pl.ds(r, v.shape[0]), :] = v

            own = lambda x, j: state[k // 3, k % 3 + c, pl.ds(x, 8), lanes(j)]
            place_field(put, own, q, x_lo, x_hi, y_lo, y_hi, low)
        return 0

    lax.fori_loop(0, 6, load, 0)
    step = half_steps(where, fe, fh, factor)
    for n in range(STEPS):

        def use(b, olds, news):
            terms = [news[i] * inc[STEPS - 1 - n, i, pl.ds(b, 8), :] for i in range(6)]
            total = ((terms[0] + terms[1]) + terms[2]) + ((terms[3] + terms[4]) + terms[5])
            if n > 0:
                total = total + density[pl.ds(b, 8), :]
            density[pl.ds(b, 8), :] = total

        step(n, use)

    for j in range(TJ // 2):
        for t in range(2):
            g = []
            for r in (2 * j + HALO, 2 * j + HALO + 1):
                at = pl.ds(r * XR + HALO + 8 * t, 8)
                g.append(density[at, :] * (factor[at, :] * (-1.0 / COURANT)))
            for tile, v in (
                (j, jnp.where(low, g[0], pltpu.roll(g[1], NZ, 1))),
                (j + TJ // 2, jnp.where(low, pltpu.roll(g[0], NZ, 1), g[1])),
            ):
                for h in range(2):
                    b = ((2 * t + h) * (TJ // 2) + tile // 2) * 8 + tile % 2
                    block[pl.ds(b, 4, stride=2), :] = v[4 * h : 4 * h + 4]
    out[...] = jnp.zeros_like(out)

    def send(i, _):
        o = owners[i]

        @pl.when(o >= 0)
        def _():
            c = pl.multiple_of(slots[i] * 4, 4)
            b = pl.multiple_of(i * 8, 8)
            out[o, pl.ds(c, 4), :] = block[pl.ds(b, 4), :]
            out[16 + o, pl.ds(c, 4), :] = block[pl.ds(b + 4, 4), :]

        return 0

    lax.fori_loop(0, 64, send, 0)


def place(rows, arrived, out, wide):
    def one(g, _):
        v = arrived[g] + arrived[16 + g]
        for c in range(4):
            r = pl.multiple_of(rows[g * 4 + c] * 4, 4)
            wide[pl.ds(r, 4), :] = v[c * 4 : c * 4 + 4]
        return 0

    lax.fori_loop(0, 16, one, 0)
    for i in range(8):
        for q in range(4):
            out[8 * i : 8 * i + 8, lanes(q)] = wide[pl.ds(32 * i + q, 8, stride=4), :]


FULL = pl.BlockSpec(memory_space=pltpu.VMEM)
SCALARS = pl.BlockSpec(memory_space=pltpu.SMEM)


def buf(*shape):
    return jax.ShapeDtypeStruct(shape, F32)


def call(kernel, n_scalars, n_arrays, outs, scratch=(), mib=24, us=2):
    return pl.pallas_call(
        kernel,
        in_specs=[SCALARS] * n_scalars + [FULL] * n_arrays,
        out_specs=[FULL] * len(outs),
        out_shape=list(outs),
        scratch_shapes=[pltpu.VMEM(shape, F32) for shape in scratch],
        compiler_params=pltpu.CompilerParams(vmem_limit_bytes=mib << 20),
        cost_estimate=pl.CostEstimate(
            flops=us * 1000000, bytes_accessed=us * 3000000, transcendentals=0
        ),
        name=kernel.__name__,
    )


def call_pack_y(n_own, count, rows):
    strip = (2, 6, CX, 2 * W)
    whole = lambda n: pl.BlockSpec((n, W), lambda i: (0, 0))
    specs = [
        pl.BlockSpec(strip, lambda i: (0, 0, 0, 0)),
        pl.BlockSpec(strip, lambda i: (0, 0, 0, TJ // 2 - 1)),
    ]
    if count == 13:
        specs += [
            pl.BlockSpec((CX, 2 * W), lambda i: (0, 0)),
            pl.BlockSpec((CX, 2 * W), lambda i: (0, TJ // 2 - 1)),
        ]
    return pl.pallas_call(
        pack_y,
        grid=(1,),
        in_specs=specs + [whole(count * TJ * 4)] * 2,
        out_specs=[whole(rows)] * 2,
        out_shape=[buf(rows, W)] * 2,
        compiler_params=pltpu.CompilerParams(vmem_limit_bytes=24 << 20),
        name="pack_y",
    )


FIELD = (6, ROWS, W)
SENT = (32, 16, W)


def call_forward():
    return call(forward, 3, 6, [buf(STEPS, *FIELD), buf(ROWS, W)], [FIELD, FIELD], 32, 15)


def call_adjoint():
    return call(adjoint, 3, 7, [buf(*SENT)], [FIELD, FIELD, (ROWS, W), (64 * 8, W)], 36, 15)


def per_device(
    forward_state,
    adjoint_state,
    permittivity,
    waveform,
    source_cell,
    block_owner,
    block_slot,
    owner_rows,
):
    gx, gy = lax.axis_index("gx"), lax.axis_index("gy")
    where = jnp.stack(
        [
            gx == 0,
            gx == lax.axis_size("gx") - 1,
            gy == 0,
            gy == lax.axis_size("gy") - 1,
            gx,
            gy,
        ]
    ).astype(jnp.int32)

    fx_up, fx_dn = call(pack_x, 0, 2, [buf(13 * TJ * 4, W)] * 2)(forward_state, permittivity)
    fx_lo, fx_hi = passed_along(fx_up, "gx", 1), passed_along(fx_dn, "gx", -1)
    ax_up, ax_dn = call(pack_x, 0, 1, [buf(12 * TJ * 4, W)] * 2)(adjoint_state)
    ax_lo, ax_hi = passed_along(ax_up, "gx", 1), passed_along(ax_dn, "gx", -1)

    fy_up, fy_dn = call_pack_y(4, 13, 13 * 2 * XR)(
        forward_state, forward_state, permittivity, permittivity, fx_lo, fx_hi
    )
    fy_lo, fy_hi = passed_along(fy_up, "gy", 1), passed_along(fy_dn, "gy", -1)
    ay_up, ay_dn = call_pack_y(2, 12, 12 * 2 * XR)(adjoint_state, adjoint_state, ax_lo, ax_hi)
    ay_lo, ay_hi = passed_along(ay_up, "gy", 1), passed_along(ay_dn, "gy", -1)

    inc, factor = call_forward()(
        where, source_cell, waveform, forward_state, permittivity, fx_lo, fx_hi, fy_lo, fy_hi
    )
    (outgoing,) = call_adjoint()(
        where,
        block_owner.reshape(-1),
        block_slot.reshape(-1),
        adjoint_state,
        factor,
        inc,
        ax_lo,
        ax_hi,
        ay_lo,
        ay_hi,
    )
    arrived = lax.all_to_all(outgoing, ("src", "gy"), 0, 0, tiled=True)
    (placed,) = call(place, 1, 1, [buf(64, 512)], [(256, W)])(owner_rows.reshape(-1), arrived)
    return placed


def solution(mesh):
    in_specs = (
        P("src", None, "gx", "gy"),
        P("src", None, "gx", "gy"),
        P("gx", "gy"),
        P("src", None),
        P("src", None),
        P("gx", "gy"),
        P("gx", "gy"),
        P(("gx", "gy"), None),
    )
    out_specs = P(("gx", "gy"), "src")
    return jax.shard_map(
        per_device, mesh=mesh, in_specs=in_specs, out_specs=out_specs, check_vma=False
    )
```

```python
import jax
import jax.numpy as jnp
from jax import lax
from jax.experimental import pallas as pl
from jax.experimental.pallas import tpu as pltpu
from jax.sharding import PartitionSpec as P

NZ = 64
STEPS = 4
HALO = 4
CX = 16
XR = CX + 2 * HALO
CY = 64
TJ = CY // 2
HY = CY // 2
TR = HY + 2 * HALO
ROWS = TR * XR
UNROLL = 4
W = 128
COURANT = 0.55
F32 = jnp.float32


def passed_along(shard, axis, by):
    count = lax.axis_size(axis)
    pairs = [(i, i + by) for i in range(count) if 0 <= i + by < count]
    return lax.ppermute(shard, axis, pairs)


def lanes(tile):
    return pl.ds(tile * W, W)


def aligned(index, step):
    return index if isinstance(index, int) else pl.multiple_of(index, step)


def pack_x(state, *rest):
    eps, up, dn = rest if len(rest) == 3 else (None, *rest)

    def put(k, get):
        for j in range(TJ):
            row = aligned((k * TJ + j) * 4, 4)
            dn[pl.ds(row, 4), :] = get(pl.ds(0, 4), lanes(j))
            up[pl.ds(row, 4), :] = get(pl.ds(CX - 4, 4), lanes(j))

    def one(k, _):
        put(k, lambda x, j: state[k // 6, k % 6, x, j])
        return 0

    lax.fori_loop(0, 12, one, 0)
    if eps is not None:
        put(12, lambda x, j: COURANT / eps[x, j])


def pack_y(own_lo, own_hi, *rest):
    eps = None
    if len(rest) == 6:
        eps, rest = rest[:2], rest[2:]
    x_lo, x_hi, up, dn = rest

    def put(k, get):
        for j in range(2):
            base = aligned((k * 2 + j) * XR, 8)
            for out, side, tile in ((dn, 0, j), (up, 1, TJ - 2 + j)):
                row = aligned((k * TJ + tile) * 4, 4)
                out[pl.ds(base, 4), :] = x_lo[pl.ds(row, 4), :]
                out[pl.ds(base + 4, CX), :] = get(side, lanes(j))
                out[pl.ds(base + 4 + CX, 4), :] = x_hi[pl.ds(row, 4), :]

    def one(k, _):
        put(k, lambda side, j: (own_lo, own_hi)[side][k // 6, k % 6, :, j])
        return 0

    lax.fori_loop(0, 12, one, 0)
    if eps is not None:
        put(12, lambda side, j: COURANT / eps[side][:, j])


def place_field(put, own, k, x_lo, x_hi, y_lo, y_hi, low):
    pieces = ((0, 4), (4, 8), (12, 8), (20, 4))

    def source(j, x, n):
        if j < 0 or j >= TJ:
            ghost, g = (y_lo, j + 2) if j < 0 else (y_hi, j - TJ)
            return ghost[pl.ds(aligned((k * 2 + g) * XR, 8) + x, n), :]
        if n == 8:
            return own(x - 4, j)
        return (x_lo if x == 0 else x_hi)[pl.ds(aligned((k * TJ + j) * 4, 4), 4), :]

    for u in range(TR // 2):
        for x, n in pieces:
            a = source(u - 2, x, n)
            b = source(u - 2 + TJ // 2, x, n)
            first = low[:n]
            put(2 * u * XR + x, jnp.where(first, a, pltpu.roll(b, NZ, 1)))
            put((2 * u + 1) * XR + x, jnp.where(first, pltpu.roll(a, NZ, 1), b))


def masks():
    lane = lax.broadcasted_iota(jnp.int32, (8, W), 1)
    return lane < NZ, (lane & (NZ - 1)) == 0, (lane & (NZ - 1)) == NZ - 1


def half_steps(where, fe, fh, factor):
    low, z_first, z_last = masks()
    row8 = lax.broadcasted_iota(jnp.int32, (8, W), 0)
    at_x0, at_x1, at_y0, at_y1 = (where[i] for i in range(4))
    coef_x = [
        jnp.where((row8 < 4) & (at_x0 == 1), 0.0, COURANT).astype(F32),
        jnp.full((8, W), COURANT, F32),
        jnp.where((row8 >= 4) & (at_x1 == 1), 0.0, COURANT).astype(F32),
    ]

    def up_z(v):
        return jnp.where(z_last, 0.0, pltpu.roll(v, W - 1, 1))

    def down_z(v):
        return jnp.where(z_first, 0.0, pltpu.roll(v, 1, 1))

    def magnetic(r):
        in_low = jnp.where((r < HALO) & (at_y0 == 1), 0.0, 1.0).astype(F32)
        in_high = jnp.where((r >= HALO + HY) & (at_y1 == 1), 0.0, 1.0).astype(F32)
        inside = jnp.where(low, in_low, in_high)
        for t in range(3):
            b = pl.multiple_of(r * XR + 8 * t, 8)
            c = coef_x[t] * inside
            for s in range(2):
                k = 3 * s
                ex = fe[k, pl.ds(b, 8), :]
                ey = fe[k + 1, pl.ds(b, 8), :]
                ez = fe[k + 2, pl.ds(b, 8), :]
                ex_y = fe[k, pl.ds(b + XR, 8), :]
                ez_y = fe[k + 2, pl.ds(b + XR, 8), :]
                ey_x = fe[k + 1, pl.ds(b + 1, 8), :]
                ez_x = fe[k + 2, pl.ds(b + 1, 8), :]
                hx = fh[k, pl.ds(b, 8), :] - c * ((ez_y - ez) - (up_z(ey) - ey))
                hy = fh[k + 1, pl.ds(b, 8), :] - c * ((up_z(ex) - ex) - (ez_x - ez))
                hz = fh[k + 2, pl.ds(b, 8), :] - c * ((ey_x - ey) - (ex_y - ex))
                fh[k, pl.ds(b, 8), :] = hx
                fh[k + 1, pl.ds(b, 8), :] = hy
                fh[k + 2, pl.ds(b, 8), :] = hz

    def electric(r, use):
        for t in range(3):
            b = pl.multiple_of(r * XR + 8 * t, 8)
            f = factor[pl.ds(b, 8), :]
            olds, news = [], []
            for s in range(2):
                k = 3 * s
                hx = fh[k, pl.ds(b, 8), :]
                hy = fh[k + 1, pl.ds(b, 8), :]
                hz = fh[k + 2, pl.ds(b, 8), :]
                hx_y = fh[k, pl.ds(b - XR, 8), :]
                hz_y = fh[k + 2, pl.ds(b - XR, 8), :]
                hy_x = fh[k + 1, pl.ds(b - 1, 8), :]
                hz_x = fh[k + 2, pl.ds(b - 1, 8), :]
                ex, ey, ez = (fe[k + c, pl.ds(b, 8), :] for c in range(3))
                nx = ex + f * ((hz - hz_y) - (hy - down_z(hy)))
                ny = ey + f * ((hx - down_z(hx)) - (hz - hz_x))
                nz = ez + f * ((hy - hy_x) - (hx - hx_y))
                fe[k, pl.ds(b, 8), :] = nx
                fe[k + 1, pl.ds(b, 8), :] = ny
                fe[k + 2, pl.ds(b, 8), :] = nz
                olds += [ex, ey, ez]
                news += [nx, ny, nz]
            use(b, olds, news)

    def over(first, last, one):
        def body(r, _):
            one(r)
            return 0

        lax.fori_loop(first, last, body, 0, unroll=UNROLL)

    def step(n, use):
        over(n, TR - 1 - n, magnetic)
        over(n + 1, TR - 1 - n, lambda r: electric(r, use))

    return step


def forward(
    where, cells, wave, state, eps, x_lo, x_hi, y_lo, y_hi, inc, factor, fe, fh
):
    low = masks()[0]

    def load(k, _):
        for ref, c in ((fe, 0), (fh, 3)):
            q = 6 * (k // 3) + k % 3 + c

            def put(r, v):
                ref[k, pl.ds(r, v.shape[0]), :] = v

            own = lambda x, j: state[k // 3, k % 3 + c, pl.ds(x, 8), lanes(j)]
            place_field(put, own, q, x_lo, x_hi, y_lo, y_hi, low)
        return 0

    lax.fori_loop(0, 6, load, 0)

    def put(r, v):
        factor[pl.ds(r, v.shape[0]), :] = v

    place_field(
        put, lambda x, j: COURANT / eps[pl.ds(x, 8), lanes(j)], 12, x_lo, x_hi, y_lo, y_hi, low
    )
    step = half_steps(where, fe, fh, factor)
    lane = lax.broadcasted_iota(jnp.int32, (1, W), 1)
    for n in range(STEPS):

        def use(b, olds, news):
            for i in range(6):
                inc[n, i, pl.ds(b, 8), :] = news[i] - olds[i]

        step(n, use)
        for s in range(2):
            x = cells[s, 0] - where[4] * CX + HALO
            y = cells[s, 1] - where[5] * CY + HALO
            for h in range(2):
                r = y - h * HY

                @pl.when((x >= 0) & (x < XR) & (r >= 0) & (r < TR))
                def _():
                    at = pl.ds(r * XR + x, 1)
                    pulse = jnp.where(lane == h * NZ + cells[s, 2], wave[s, n], 0.0).astype(F32)
                    fe[3 * s + 2, at, :] += pulse
                    inc[n, 3 * s + 2, at, :] += pulse


def adjoint(
    where, owners, slots, state, factor, inc, x_lo, x_hi, y_lo, y_hi, out, fe, fh, density, block
):
    low = masks()[0]

    def load(k, _):
        for ref, c in ((fe, 0), (fh, 3)):
            q = 6 * (k // 3) + k % 3 + c

            def put(r, v):
                ref[k, pl.ds(r, v.shape[0]), :] = v

            own = lambda x, j: state[k // 3, k % 3 + c, pl.ds(x, 8), lanes(j)]
            place_field(put, own, q, x_lo, x_hi, y_lo, y_hi, low)
        return 0

    lax.fori_loop(0, 6, load, 0)
    step = half_steps(where, fe, fh, factor)
    for n in range(STEPS):

        def use(b, olds, news):
            terms = [news[i] * inc[STEPS - 1 - n, i, pl.ds(b, 8), :] for i in range(6)]
            total = ((terms[0] + terms[1]) + terms[2]) + ((terms[3] + terms[4]) + terms[5])
            if n > 0:
                total = total + density[pl.ds(b, 8), :]
            density[pl.ds(b, 8), :] = total

        step(n, use)

    for j in range(TJ // 2):
        for t in range(2):
            g = []
            for r in (2 * j + HALO, 2 * j + HALO + 1):
                at = pl.ds(r * XR + HALO + 8 * t, 8)
                g.append(density[at, :] * (factor[at, :] * (-1.0 / COURANT)))
            for tile, v in (
                (j, jnp.where(low, g[0], pltpu.roll(g[1], NZ, 1))),
                (j + TJ // 2, jnp.where(low, pltpu.roll(g[0], NZ, 1), g[1])),
            ):
                for h in range(2):
                    b = ((2 * t + h) * (TJ // 2) + tile // 2) * 8 + tile % 2
                    block[pl.ds(b, 4, stride=2), :] = v[4 * h : 4 * h + 4]
    out[...] = jnp.zeros_like(out)

    def send(i, _):
        o = owners[i]

        @pl.when(o >= 0)
        def _():
            c = pl.multiple_of(slots[i] * 4, 4)
            b = pl.multiple_of(i * 8, 8)
            out[o, pl.ds(c, 4), :] = block[pl.ds(b, 4), :]
            out[16 + o, pl.ds(c, 4), :] = block[pl.ds(b + 4, 4), :]

        return 0

    lax.fori_loop(0, 64, send, 0)


def place(rows, arrived, out, wide):
    def one(g, _):
        v = arrived[g] + arrived[16 + g]
        for c in range(4):
            r = pl.multiple_of(rows[g * 4 + c] * 4, 4)
            wide[pl.ds(r, 4), :] = v[c * 4 : c * 4 + 4]
        return 0

    lax.fori_loop(0, 16, one, 0)
    for i in range(8):
        for q in range(4):
            out[8 * i : 8 * i + 8, lanes(q)] = wide[pl.ds(32 * i + q, 8, stride=4), :]


FULL = pl.BlockSpec(memory_space=pltpu.VMEM)
SCALARS = pl.BlockSpec(memory_space=pltpu.SMEM)


def buf(*shape):
    return jax.ShapeDtypeStruct(shape, F32)


def call(kernel, n_scalars, n_arrays, outs, scratch=(), mib=8, us=2):
    return pl.pallas_call(
        kernel,
        in_specs=[SCALARS] * n_scalars + [FULL] * n_arrays,
        out_specs=[FULL] * len(outs),
        out_shape=list(outs),
        scratch_shapes=[pltpu.VMEM(shape, F32) for shape in scratch],
        compiler_params=pltpu.CompilerParams(vmem_limit_bytes=mib << 20),
        cost_estimate=pl.CostEstimate(
            flops=us * 1000000, bytes_accessed=us * 3000000, transcendentals=0
        ),
        name=kernel.__name__,
    )


def call_pack_y(n_own, count, rows):
    strip = (2, 6, CX, 2 * W)
    whole = lambda n: pl.BlockSpec((n, W), lambda i: (0, 0))
    specs = [
        pl.BlockSpec(strip, lambda i: (0, 0, 0, 0)),
        pl.BlockSpec(strip, lambda i: (0, 0, 0, TJ // 2 - 1)),
    ]
    if count == 13:
        specs += [
            pl.BlockSpec((CX, 2 * W), lambda i: (0, 0)),
            pl.BlockSpec((CX, 2 * W), lambda i: (0, TJ // 2 - 1)),
        ]
    return pl.pallas_call(
        pack_y,
        grid=(1,),
        in_specs=specs + [whole(count * TJ * 4)] * 2,
        out_specs=[whole(rows)] * 2,
        out_shape=[buf(rows, W)] * 2,
        compiler_params=pltpu.CompilerParams(vmem_limit_bytes=8 << 20),
        name="pack_y",
    )


FIELD = (6, ROWS, W)
SENT = (32, 16, W)


def call_forward():
    return call(forward, 3, 6, [buf(STEPS, *FIELD), buf(ROWS, W)], [FIELD, FIELD], 12, 15)


def call_adjoint():
    return call(adjoint, 3, 7, [buf(*SENT)], [FIELD, FIELD, (ROWS, W), (64 * 8, W)], 12, 15)


def per_device(
    forward_state,
    adjoint_state,
    permittivity,
    waveform,
    source_cell,
    block_owner,
    block_slot,
    owner_rows,
):
    gx, gy = lax.axis_index("gx"), lax.axis_index("gy")
    where = jnp.stack(
        [
            gx == 0,
            gx == lax.axis_size("gx") - 1,
            gy == 0,
            gy == lax.axis_size("gy") - 1,
            gx,
            gy,
        ]
    ).astype(jnp.int32)

    fx_up, fx_dn = call(pack_x, 0, 2, [buf(13 * TJ * 4, W)] * 2)(forward_state, permittivity)
    fx_lo, fx_hi = passed_along(fx_up, "gx", 1), passed_along(fx_dn, "gx", -1)
    ax_up, ax_dn = call(pack_x, 0, 1, [buf(12 * TJ * 4, W)] * 2)(adjoint_state)
    ax_lo, ax_hi = passed_along(ax_up, "gx", 1), passed_along(ax_dn, "gx", -1)

    fy_up, fy_dn = call_pack_y(4, 13, 13 * 2 * XR)(
        forward_state, forward_state, permittivity, permittivity, fx_lo, fx_hi
    )
    fy_lo, fy_hi = passed_along(fy_up, "gy", 1), passed_along(fy_dn, "gy", -1)
    ay_up, ay_dn = call_pack_y(2, 12, 12 * 2 * XR)(adjoint_state, adjoint_state, ax_lo, ax_hi)
    ay_lo, ay_hi = passed_along(ay_up, "gy", 1), passed_along(ay_dn, "gy", -1)

    inc, factor = call_forward()(
        where, source_cell, waveform, forward_state, permittivity, fx_lo, fx_hi, fy_lo, fy_hi
    )
    (outgoing,) = call_adjoint()(
        where,
        block_owner.reshape(-1),
        block_slot.reshape(-1),
        adjoint_state,
        factor,
        inc,
        ax_lo,
        ax_hi,
        ay_lo,
        ay_hi,
    )
    arrived = lax.all_to_all(outgoing, ("src", "gy"), 0, 0, tiled=True)
    (placed,) = call(place, 1, 1, [buf(64, 512)], [(256, W)])(owner_rows.reshape(-1), arrived)
    return placed


def solution(mesh):
    in_specs = (
        P("src", None, "gx", "gy"),
        P("src", None, "gx", "gy"),
        P("gx", "gy"),
        P("src", None),
        P("src", None),
        P("gx", "gy"),
        P("gx", "gy"),
        P(("gx", "gy"), None),
    )
    out_specs = P(("gx", "gy"), "src")
    return jax.shard_map(
        per_device, mesh=mesh, in_specs=in_specs, out_specs=out_specs, check_vma=False
    )
```

```python
import jax
import jax.numpy as jnp
from jax import lax
from jax.experimental import pallas as pl
from jax.experimental.pallas import tpu as pltpu
from jax.sharding import PartitionSpec as P

NZ = 64
STEPS = 4
HALO = 4
CX = 16
XR = CX + 2 * HALO
CY = 64
TJ = CY // 2
HY = CY // 2
TR = HY + 2 * HALO
TE = TJ + 4
ROWS = TR * XR
UNROLL = 6
W = 128
COURANT = 0.55
F32 = jnp.float32


def swapped(far, near, axis):
    count = lax.axis_size(axis)
    out = []
    for shard, first in ((near, 0), (far, 1)):
        pairs = [(i, i + 1) for i in range(first, count - 1, 2)]
        out.append(lax.ppermute(shard, axis, pairs + [(j, i) for i, j in pairs]))
    return out[0], out[1]


def lanes(tile):
    return pl.ds(tile * W, W)


def aligned(index, step):
    return index if isinstance(index, int) else pl.multiple_of(index, step)


def odd(axis):
    return lax.axis_index(axis) & 1


def pack_y(fwd, adj, eps, far, near, rim, sems):
    at = (1 - odd("gy")) * (TJ - 2)
    copies = []
    for i, (out, tile) in enumerate(((far, TJ - 2 - at), (near, at))):
        where = pl.ds(pl.multiple_of(tile * W, W), 2 * W)
        copies.append(pltpu.make_async_copy(eps.at[:, where], rim.at[i], sems.at[i, 4]))
        for n in range(4):
            state, src = (fwd, adj)[n // 2], n % 2
            copies.append(
                pltpu.make_async_copy(
                    state.at[src, :, :, where], out.at[pl.ds(6 * n, 6)], sems.at[i, n]
                )
            )
    for copy in copies:
        copy.start()
    for i, out in enumerate((far, near)):
        copies[5 * i].wait()
        out[24] = COURANT / rim[i]
    for copy in copies[1:5] + copies[6:]:
        copy.wait()


def to_halves(own, put, low):
    for u in range(TR // 2):
        for x in (0, 8):
            a = own(x, u - 2) if u >= 2 else jnp.zeros((8, W), F32)
            b = own(x, u + 14) if u + 14 < TJ else jnp.zeros((8, W), F32)
            put(2 * u * CX + x, jnp.where(low, a, pltpu.roll(b, NZ, 1)))
            put((2 * u + 1) * CX + x, jnp.where(low, pltpu.roll(a, NZ, 1), b))


def convert(state, *rest):
    eps, e, h, factor = rest if len(rest) == 4 else (None, *rest, None)
    low = masks()[0]

    def one(k, _):
        for ref, c in ((e, 0), (h, 3)):

            def put(r, v):
                ref[k, pl.ds(r, 8), :] = v

            to_halves(lambda x, j: state[k // 3, k % 3 + c, x : x + 8, lanes(j)], put, low)
        return 0

    lax.fori_loop(0, 6, one, 0)
    if eps is not None:

        def put(r, v):
            factor[pl.ds(r, 8), :] = v

        to_halves(lambda x, j: COURANT / eps[x : x + 8, lanes(j)], put, low)


def pack_x(first, state, *rest):
    eps, y_far, y_near, far, near = rest if len(rest) == 5 else (None, *rest)

    def fill(lo, hi, dn, up):
        def put(k, q, get):
            for j in range(TE):
                row = aligned((k * TE + j) * 4, 4)
                for out, x in ((dn, 0), (up, CX - 4)):
                    if j < 2:
                        v = lo[q, x : x + 4, lanes(j)]
                    elif j >= TE - 2:
                        v = hi[q, x : x + 4, lanes(j - TE + 2)]
                    else:
                        v = get(x, lanes(j - 2))
                    out[pl.ds(row, 4), :] = v

        def one(k, _):
            put(k, first + k, lambda x, j: state[k // 6, k % 6, x : x + 4, j])
            return 0

        lax.fori_loop(0, 12, one, 0)
        if eps is not None:
            put(12, 24, lambda x, j: COURANT / eps[x : x + 4, j])

    for px in range(2):
        for py in range(2):

            @pl.when((odd("gx") == px) & (odd("gy") == py))
            def _():
                ghosts = (y_far, y_near) if py == 0 else (y_near, y_far)
                outs = (far, near) if px == 0 else (near, far)
                fill(*ghosts, *outs)


def place_field(put, own, k, xg, yg, low):
    def from_x(side, j):
        return xg[side, pl.ds(aligned((k * TE + j + 2) * 4, 4), 4), :]

    for u in range(TR // 2):
        for side, x in ((0, 0), (1, HALO + CX)):
            a, b = from_x(side, u - 2), from_x(side, u - 2 + TJ // 2)
            put(2 * u * XR + x, jnp.where(low[:4], a, pltpu.roll(b, NZ, 1)))
            put((2 * u + 1) * XR + x, jnp.where(low[:4], pltpu.roll(a, NZ, 1), b))
        for x in (0, 8):
            for r in (2 * u, 2 * u + 1):
                v = own(pl.ds(r * CX + x, 8))
                if u < 2 or u >= TR // 2 - 2:
                    below = u < 2
                    g = yg[int(not below), k, pl.ds(x, 8), lanes(u if below else u - TR // 2 + 2)]
                    if below == bool(r % 2):
                        g = pltpu.roll(g, NZ, 1)
                    v = jnp.where(low, g, v) if below else jnp.where(low, v, g)
                put(r * XR + HALO + x, v)


def order_ghosts(x_near, x_far, y_near, y_far, first, count, xg, yg):
    px, py = odd("gx"), odd("gy")
    xg[1 - px] = x_near[...]
    xg[px] = x_far[...]
    yg[1 - py, 0:12] = y_near[first : first + 12]
    yg[py, 0:12] = y_far[first : first + 12]
    if count == 13:
        yg[1 - py, 12] = y_near[24]
        yg[py, 12] = y_far[24]


def masks():
    lane = lax.broadcasted_iota(jnp.int32, (8, W), 1)
    return lane < NZ, (lane & (NZ - 1)) == 0, (lane & (NZ - 1)) == NZ - 1


def half_steps(fe, fh, factor):
    low, z_first, z_last = masks()
    row8 = lax.broadcasted_iota(jnp.int32, (8, W), 0)
    gx, gy = lax.axis_index("gx"), lax.axis_index("gy")
    at_x0, at_x1 = gx == 0, gx == lax.axis_size("gx") - 1
    at_y0, at_y1 = gy == 0, gy == lax.axis_size("gy") - 1
    coef_x = [
        jnp.where((row8 < 4) & at_x0, 0.0, COURANT).astype(F32),
        jnp.full((8, W), COURANT, F32),
        jnp.where((row8 >= 4) & at_x1, 0.0, COURANT).astype(F32),
    ]

    def up_z(v):
        return jnp.where(z_last, 0.0, pltpu.roll(v, W - 1, 1))

    def down_z(v):
        return jnp.where(z_first, 0.0, pltpu.roll(v, 1, 1))

    def magnetic(r):
        in_low = jnp.where((r < HALO) & at_y0, 0.0, 1.0).astype(F32)
        in_high = jnp.where((r >= HALO + HY) & at_y1, 0.0, 1.0).astype(F32)
        inside = jnp.where(low, in_low, in_high)
        for t in range(3):
            b = pl.multiple_of(r * XR + 8 * t, 8)
            c = coef_x[t] * inside
            for s in range(2):
                k = 3 * s
                ex = fe[k, pl.ds(b, 8), :]
                ey = fe[k + 1, pl.ds(b, 8), :]
                ez = fe[k + 2, pl.ds(b, 8), :]
                ex_y = fe[k, pl.ds(b + XR, 8), :]
                ez_y = fe[k + 2, pl.ds(b + XR, 8), :]
                ey_x = fe[k + 1, pl.ds(b + 1, 8), :]
                ez_x = fe[k + 2, pl.ds(b + 1, 8), :]
                hx = fh[k, pl.ds(b, 8), :] - c * ((ez_y - ez) - (up_z(ey) - ey))
                hy = fh[k + 1, pl.ds(b, 8), :] - c * ((up_z(ex) - ex) - (ez_x - ez))
                hz = fh[k + 2, pl.ds(b, 8), :] - c * ((ey_x - ey) - (ex_y - ex))
                fh[k, pl.ds(b, 8), :] = hx
                fh[k + 1, pl.ds(b, 8), :] = hy
                fh[k + 2, pl.ds(b, 8), :] = hz

    def electric(r, use):
        for t in range(3):
            b = pl.multiple_of(r * XR + 8 * t, 8)
            f = factor[pl.ds(b, 8), :]
            olds, news = [], []
            for s in range(2):
                k = 3 * s
                hx = fh[k, pl.ds(b, 8), :]
                hy = fh[k + 1, pl.ds(b, 8), :]
                hz = fh[k + 2, pl.ds(b, 8), :]
                hx_y = fh[k, pl.ds(b - XR, 8), :]
                hz_y = fh[k + 2, pl.ds(b - XR, 8), :]
                hy_x = fh[k + 1, pl.ds(b - 1, 8), :]
                hz_x = fh[k + 2, pl.ds(b - 1, 8), :]
                ex, ey, ez = (fe[k + c, pl.ds(b, 8), :] for c in range(3))
                nx = ex + f * ((hz - hz_y) - (hy - down_z(hy)))
                ny = ey + f * ((hx - down_z(hx)) - (hz - hz_x))
                nz = ez + f * ((hy - hy_x) - (hx - hx_y))
                fe[k, pl.ds(b, 8), :] = nx
                fe[k + 1, pl.ds(b, 8), :] = ny
                fe[k + 2, pl.ds(b, 8), :] = nz
                olds += [ex, ey, ez]
                news += [nx, ny, nz]
            use(b, olds, news)

    def over(first, last, one):
        def body(r, _):
            one(r)
            return 0

        lax.fori_loop(first, last, body, 0, unroll=UNROLL)

    def step(n, use):
        over(n, TR - 1 - n, magnetic)
        over(n + 1, TR - 1 - n, lambda r: electric(r, use))

    return step


def forward(
    cells,
    wave,
    own_e,
    own_h,
    own_f,
    x_far,
    x_near,
    y_far,
    y_near,
    inc,
    factor,
    fe,
    fh,
    xg,
    yg,
):
    low = masks()[0]
    order_ghosts(x_near, x_far, y_near, y_far, 0, 13, xg, yg)

    def load(k, _):
        for ref, own, c in ((fe, own_e, 0), (fh, own_h, 3)):
            q = 6 * (k // 3) + k % 3 + c

            def put(r, v):
                ref[k, pl.ds(r, v.shape[0]), :] = v

            place_field(put, lambda at: own[k, at, :], q, xg, yg, low)
        return 0

    lax.fori_loop(0, 6, load, 0)

    def put(r, v):
        factor[pl.ds(r, v.shape[0]), :] = v

    place_field(put, lambda at: own_f[at, :], 12, xg, yg, low)
    step = half_steps(fe, fh, factor)
    lane = lax.broadcasted_iota(jnp.int32, (1, W), 1)
    for n in range(STEPS):

        def use(b, olds, news):
            for i in range(6):
                inc[n, i, pl.ds(b, 8), :] = news[i] - olds[i]

        step(n, use)
        for s in range(2):
            x = cells[s, 0] - lax.axis_index("gx") * CX + HALO
            y = cells[s, 1] - lax.axis_index("gy") * CY + HALO
            for h in range(2):
                r = y - h * HY

                @pl.when((x >= 0) & (x < XR) & (r >= 0) & (r < TR))
                def _():
                    at = pl.ds(r * XR + x, 1)
                    pulse = jnp.where(lane == h * NZ + cells[s, 2], wave[s, n], 0.0).astype(F32)
                    fe[3 * s + 2, at, :] += pulse
                    inc[n, 3 * s + 2, at, :] += pulse


def adjoint(
    owners,
    slots,
    own_e,
    own_h,
    factor,
    inc,
    x_far,
    x_near,
    y_far,
    y_near,
    out,
    fe,
    fh,
    xg,
    yg,
    density,
    block,
):
    low = masks()[0]
    order_ghosts(x_near, x_far, y_near, y_far, 12, 12, xg, yg)

    def load(k, _):
        for ref, own, c in ((fe, own_e, 0), (fh, own_h, 3)):
            q = 6 * (k // 3) + k % 3 + c

            def put(r, v):
                ref[k, pl.ds(r, v.shape[0]), :] = v

            place_field(put, lambda at: own[k, at, :], q, xg, yg, low)
        return 0

    lax.fori_loop(0, 6, load, 0)
    step = half_steps(fe, fh, factor)
    for n in range(STEPS):

        def use(b, olds, news):
            terms = [news[i] * inc[STEPS - 1 - n, i, pl.ds(b, 8), :] for i in range(6)]
            total = ((terms[0] + terms[1]) + terms[2]) + ((terms[3] + terms[4]) + terms[5])
            if n > 0:
                total = total + density[pl.ds(b, 8), :]
            density[pl.ds(b, 8), :] = total

        step(n, use)

    for j in range(TJ // 2):
        for t in range(2):
            g = []
            for r in (2 * j + HALO, 2 * j + HALO + 1):
                at = pl.ds(r * XR + HALO + 8 * t, 8)
                g.append(density[at, :] * (factor[at, :] * (-1.0 / COURANT)))
            for tile, v in (
                (j, jnp.where(low, g[0], pltpu.roll(g[1], NZ, 1))),
                (j + TJ // 2, jnp.where(low, pltpu.roll(g[0], NZ, 1), g[1])),
            ):
                for h in range(2):
                    b = ((2 * t + h) * (TJ // 2) + tile // 2) * 8 + tile % 2
                    block[pl.ds(b, 4, stride=2), :] = v[4 * h : 4 * h + 4]
    out[...] = jnp.zeros_like(out)

    def send(i, _):
        o = owners[i // 16, i % 16]

        @pl.when(o >= 0)
        def _():
            c = pl.multiple_of(slots[i // 16, i % 16] * 4, 4)
            b = pl.multiple_of(i * 8, 8)
            out[o, pl.ds(c, 4), :] = block[pl.ds(b, 4), :]
            out[16 + o, pl.ds(c, 4), :] = block[pl.ds(b + 4, 4), :]

        return 0

    lax.fori_loop(0, 64, send, 0)


def place(rows, arrived, out, wide):
    def one(g, _):
        v = arrived[g] + arrived[16 + g]
        for c in range(4):
            r = pl.multiple_of(rows[0, g * 4 + c] * 4, 4)
            wide[pl.ds(r, 4), :] = v[c * 4 : c * 4 + 4]
        return 0

    lax.fori_loop(0, 16, one, 0)
    for i in range(8):
        for q in range(4):
            out[8 * i : 8 * i + 8, lanes(q)] = wide[pl.ds(32 * i + q, 8, stride=4), :]


FULL = pl.BlockSpec(memory_space=pltpu.VMEM)
SCALARS = pl.BlockSpec(memory_space=pltpu.SMEM)


def buf(*shape):
    return jax.ShapeDtypeStruct(shape, F32)


def call(kernel, n_scalars, n_arrays, outs, scratch=(), mib=8, us=2):
    return pl.pallas_call(
        kernel,
        in_specs=[SCALARS] * n_scalars + [FULL] * n_arrays,
        out_specs=[FULL] * len(outs),
        out_shape=list(outs),
        scratch_shapes=[pltpu.VMEM(shape, F32) for shape in scratch],
        compiler_params=pltpu.CompilerParams(vmem_limit_bytes=mib << 20),
        cost_estimate=pl.CostEstimate(
            flops=us * 1000000, bytes_accessed=us * 3000000, transcendentals=0
        ),
        name=kernel.__name__,
    )


RIM = (25, CX, 2 * W)


def call_pack_y():
    hbm = pl.BlockSpec(memory_space=pltpu.HBM)
    return pl.pallas_call(
        pack_y,
        in_specs=[hbm] * 3,
        out_specs=[FULL] * 2,
        out_shape=[buf(*RIM)] * 2,
        scratch_shapes=[pltpu.VMEM((2, CX, 2 * W), F32), pltpu.SemaphoreType.DMA((2, 5))],
        compiler_params=pltpu.CompilerParams(vmem_limit_bytes=62 << 20),
        name="pack_y",
    )


def call_pack_x(first, count):
    def kernel(*refs):
        pack_x(first, *refs)

    kernel.__name__ = "pack_x"
    return call(kernel, 0, 3 + (count == 13), [buf(count * TE * 4, W)] * 2, us=1)


FIELD = (6, ROWS, W)
SENT = (32, 16, W)


def call_forward():
    ghosts = [(2, 13 * TE * 4, W), (2, 13, CX, 2 * W)]
    return call(
        forward, 2, 7, [buf(STEPS, *FIELD), buf(ROWS, W)], [FIELD, FIELD, *ghosts], 12, 15
    )


def call_adjoint():
    ghosts = [(2, 12 * TE * 4, W), (2, 12, CX, 2 * W)]
    return call(
        adjoint,
        2,
        8,
        [buf(*SENT)],
        [FIELD, FIELD, *ghosts, (ROWS, W), (64 * 8, W)],
        12,
        15,
    )


def per_device(
    forward_state,
    adjoint_state,
    permittivity,
    waveform,
    source_cell,
    block_owner,
    block_slot,
    owner_rows,
):
    y_near, y_far = swapped(
        *call_pack_y()(forward_state, adjoint_state, permittivity), "gy"
    )
    own = [buf(6, TR * CX, W)] * 2
    forward_own = call(convert, 0, 2, [*own, buf(TR * CX, W)])(forward_state, permittivity)
    adjoint_own = call(convert, 0, 1, own)(adjoint_state)
    y_near, y_far, forward_own, adjoint_own = lax.optimization_barrier(
        (y_near, y_far, forward_own, adjoint_own)
    )
    fx_near, fx_far = swapped(
        *call_pack_x(0, 13)(forward_state, permittivity, y_far, y_near), "gx"
    )
    ax_near, ax_far = swapped(*call_pack_x(12, 12)(adjoint_state, y_far, y_near), "gx")
    inc, factor = call_forward()(
        source_cell, waveform, *forward_own, fx_far, fx_near, y_far, y_near
    )
    (outgoing,) = call_adjoint()(
        block_owner,
        block_slot,
        *adjoint_own,
        factor,
        inc,
        ax_far,
        ax_near,
        y_far,
        y_near,
    )
    arrived = lax.all_to_all(outgoing, ("src", "gy"), 0, 0, tiled=True)
    (placed,) = call(place, 1, 1, [buf(64, 512)], [(256, W)])(owner_rows, arrived)
    return placed


def solution(mesh):
    in_specs = (
        P("src", None, "gx", "gy"),
        P("src", None, "gx", "gy"),
        P("gx", "gy"),
        P("src", None),
        P("src", None),
        P("gx", "gy"),
        P("gx", "gy"),
        P(("gx", "gy"), None),
    )
    out_specs = P(("gx", "gy"), "src")
    return jax.shard_map(
        per_device, mesh=mesh, in_specs=in_specs, out_specs=out_specs, check_vma=False
    )
```

```python
import jax
import jax.numpy as jnp
from jax import lax
from jax.experimental import pallas as pl
from jax.experimental.pallas import tpu as pltpu
from jax.sharding import PartitionSpec as P

NZ = 64
STEPS = 4
HALO = 4
CX = 16
XR = CX + 2 * HALO
CY = 64
TJ = CY // 2
HY = CY // 2
TR = HY + 2 * HALO
TE = TJ + 4
ROWS = TR * XR
UNROLL = 6
W = 128
COURANT = 0.55
F32 = jnp.float32


def swapped(far, near, axis):
    count = lax.axis_size(axis)
    out = []
    for shard, first in ((near, 0), (far, 1)):
        pairs = [(i, i + 1) for i in range(first, count - 1, 2)]
        out.append(lax.ppermute(shard, axis, pairs + [(j, i) for i, j in pairs]))
    return out[0], out[1]


def lanes(tile):
    return pl.ds(tile * W, W)


def aligned(index, step):
    return index if isinstance(index, int) else pl.multiple_of(index, step)


def odd(axis):
    return lax.axis_index(axis) & 1


def pack_y(fwd, adj, eps, far, near, rim, sems):
    at = (1 - odd("gy")) * (TJ - 2)
    copies = []
    for i, (out, tile) in enumerate(((far, TJ - 2 - at), (near, at))):
        where = pl.ds(pl.multiple_of(tile * W, W), 2 * W)
        copies.append(pltpu.make_async_copy(eps.at[:, where], rim.at[i], sems.at[i, 4]))
        for n in range(4):
            state, src = (fwd, adj)[n // 2], n % 2
            copies.append(
                pltpu.make_async_copy(
                    state.at[src, :, :, where], out.at[pl.ds(6 * n, 6)], sems.at[i, n]
                )
            )
    for copy in copies:
        copy.start()
    for i, out in enumerate((far, near)):
        copies[5 * i].wait()
        out[24] = COURANT / rim[i]
    for copy in copies[1:5] + copies[6:]:
        copy.wait()


def to_halves(own, put, low):
    for u in range(TR // 2):
        for x in (0, 8):
            a = own(x, u - 2) if u >= 2 else jnp.zeros((8, W), F32)
            b = own(x, u + 14) if u + 14 < TJ else jnp.zeros((8, W), F32)
            put(2 * u * CX + x, jnp.where(low, a, pltpu.roll(b, NZ, 1)))
            put((2 * u + 1) * CX + x, jnp.where(low, pltpu.roll(a, NZ, 1), b))


def convert(state, *rest):
    eps, e, h, factor = rest if len(rest) == 4 else (None, *rest, None)
    low = masks()[0]

    def one(k, _):
        for ref, c in ((e, 0), (h, 3)):

            def put(r, v):
                ref[k, pl.ds(r, 8), :] = v

            to_halves(lambda x, j: state[k // 3, k % 3 + c, x : x + 8, lanes(j)], put, low)
        return 0

    lax.fori_loop(0, 6, one, 0)
    if eps is not None:

        def put(r, v):
            factor[pl.ds(r, 8), :] = v

        to_halves(lambda x, j: COURANT / eps[x : x + 8, lanes(j)], put, low)


def pack_x(first, state, *rest):
    eps, y_far, y_near, far, near = rest if len(rest) == 5 else (None, *rest)

    def fill(lo, hi, dn, up):
        def put(k, q, get):
            for j in range(TE):
                row = aligned((k * TE + j) * 4, 4)
                for out, x in ((dn, 0), (up, CX - 4)):
                    if j < 2:
                        v = lo[q, x : x + 4, lanes(j)]
                    elif j >= TE - 2:
                        v = hi[q, x : x + 4, lanes(j - TE + 2)]
                    else:
                        v = get(x, lanes(j - 2))
                    out[pl.ds(row, 4), :] = v

        def one(k, _):
            put(k, first + k, lambda x, j: state[k // 6, k % 6, x : x + 4, j])
            return 0

        lax.fori_loop(0, 12, one, 0)
        if eps is not None:
            put(12, 24, lambda x, j: COURANT / eps[x : x + 4, j])

    for px in range(2):
        for py in range(2):

            @pl.when((odd("gx") == px) & (odd("gy") == py))
            def _():
                ghosts = (y_far, y_near) if py == 0 else (y_near, y_far)
                outs = (far, near) if px == 0 else (near, far)
                fill(*ghosts, *outs)


def place_field(put, own, k, xg, yg, low):
    def from_x(side, j):
        return xg[side, pl.ds(aligned((k * TE + j + 2) * 4, 4), 4), :]

    for u in range(TR // 2):
        for side, x in ((0, 0), (1, HALO + CX)):
            a, b = from_x(side, u - 2), from_x(side, u - 2 + TJ // 2)
            put(2 * u * XR + x, jnp.where(low[:4], a, pltpu.roll(b, NZ, 1)))
            put((2 * u + 1) * XR + x, jnp.where(low[:4], pltpu.roll(a, NZ, 1), b))
        for x in (0, 8):
            for r in (2 * u, 2 * u + 1):
                v = own(pl.ds(r * CX + x, 8))
                if u < 2 or u >= TR // 2 - 2:
                    below = u < 2
                    g = yg[int(not below), k, pl.ds(x, 8), lanes(u if below else u - TR // 2 + 2)]
                    if below == bool(r % 2):
                        g = pltpu.roll(g, NZ, 1)
                    v = jnp.where(low, g, v) if below else jnp.where(low, v, g)
                put(r * XR + HALO + x, v)


def order_ghosts(x_near, x_far, y_near, y_far, first, count, xg, yg):
    px, py = odd("gx"), odd("gy")
    xg[1 - px] = x_near[...]
    xg[px] = x_far[...]
    yg[1 - py, 0:12] = y_near[first : first + 12]
    yg[py, 0:12] = y_far[first : first + 12]
    if count == 13:
        yg[1 - py, 12] = y_near[24]
        yg[py, 12] = y_far[24]


def masks():
    lane = lax.broadcasted_iota(jnp.int32, (8, W), 1)
    return lane < NZ, (lane & (NZ - 1)) == 0, (lane & (NZ - 1)) == NZ - 1


def half_steps(fe, fh, factor):
    low, z_first, z_last = masks()
    row8 = lax.broadcasted_iota(jnp.int32, (8, W), 0)
    gx, gy = lax.axis_index("gx"), lax.axis_index("gy")
    at_x0, at_x1 = gx == 0, gx == lax.axis_size("gx") - 1
    at_y0, at_y1 = gy == 0, gy == lax.axis_size("gy") - 1
    coef_x = [
        jnp.where((row8 < 4) & at_x0, 0.0, COURANT).astype(F32),
        jnp.full((8, W), COURANT, F32),
        jnp.where((row8 >= 4) & at_x1, 0.0, COURANT).astype(F32),
    ]

    def up_z(v):
        return jnp.where(z_last, 0.0, pltpu.roll(v, W - 1, 1))

    def down_z(v):
        return jnp.where(z_first, 0.0, pltpu.roll(v, 1, 1))

    def magnetic(r):
        in_low = jnp.where((r < HALO) & at_y0, 0.0, 1.0).astype(F32)
        in_high = jnp.where((r >= HALO + HY) & at_y1, 0.0, 1.0).astype(F32)
        inside = jnp.where(low, in_low, in_high)
        for t in range(3):
            b = pl.multiple_of(r * XR + 8 * t, 8)
            c = coef_x[t] * inside
            for s in range(2):
                k = 3 * s
                ex = fe[k, pl.ds(b, 8), :]
                ey = fe[k + 1, pl.ds(b, 8), :]
                ez = fe[k + 2, pl.ds(b, 8), :]
                ex_y = fe[k, pl.ds(b + XR, 8), :]
                ez_y = fe[k + 2, pl.ds(b + XR, 8), :]
                ey_x = fe[k + 1, pl.ds(b + 1, 8), :]
                ez_x = fe[k + 2, pl.ds(b + 1, 8), :]
                hx = fh[k, pl.ds(b, 8), :] - c * ((ez_y - ez) - (up_z(ey) - ey))
                hy = fh[k + 1, pl.ds(b, 8), :] - c * ((up_z(ex) - ex) - (ez_x - ez))
                hz = fh[k + 2, pl.ds(b, 8), :] - c * ((ey_x - ey) - (ex_y - ex))
                fh[k, pl.ds(b, 8), :] = hx
                fh[k + 1, pl.ds(b, 8), :] = hy
                fh[k + 2, pl.ds(b, 8), :] = hz

    def electric(r, use):
        for t in range(3):
            b = pl.multiple_of(r * XR + 8 * t, 8)
            f = factor[pl.ds(b, 8), :]
            olds, news = [], []
            for s in range(2):
                k = 3 * s
                hx = fh[k, pl.ds(b, 8), :]
                hy = fh[k + 1, pl.ds(b, 8), :]
                hz = fh[k + 2, pl.ds(b, 8), :]
                hx_y = fh[k, pl.ds(b - XR, 8), :]
                hz_y = fh[k + 2, pl.ds(b - XR, 8), :]
                hy_x = fh[k + 1, pl.ds(b - 1, 8), :]
                hz_x = fh[k + 2, pl.ds(b - 1, 8), :]
                ex, ey, ez = (fe[k + c, pl.ds(b, 8), :] for c in range(3))
                nx = ex + f * ((hz - hz_y) - (hy - down_z(hy)))
                ny = ey + f * ((hx - down_z(hx)) - (hz - hz_x))
                nz = ez + f * ((hy - hy_x) - (hx - hx_y))
                fe[k, pl.ds(b, 8), :] = nx
                fe[k + 1, pl.ds(b, 8), :] = ny
                fe[k + 2, pl.ds(b, 8), :] = nz
                olds += [ex, ey, ez]
                news += [nx, ny, nz]
            use(b, olds, news)

    def over(first, last, one):
        def body(r, _):
            one(r)
            return 0

        lax.fori_loop(first, last, body, 0, unroll=UNROLL)

    def step(n, use):
        over(n, TR - 1 - n, magnetic)
        over(n + 1, TR - 1 - n, lambda r: electric(r, use))

    return step


def forward(
    cells,
    wave,
    own_e,
    own_h,
    own_f,
    x_far,
    x_near,
    y_far,
    y_near,
    inc,
    factor,
    fe,
    fh,
    xg,
    yg,
):
    low = masks()[0]
    order_ghosts(x_near, x_far, y_near, y_far, 0, 13, xg, yg)

    def load(k, _):
        for ref, own, c in ((fe, own_e, 0), (fh, own_h, 3)):
            q = 6 * (k // 3) + k % 3 + c

            def put(r, v):
                ref[k, pl.ds(r, v.shape[0]), :] = v

            place_field(put, lambda at: own[k, at, :], q, xg, yg, low)
        return 0

    lax.fori_loop(0, 6, load, 0)

    def put(r, v):
        factor[pl.ds(r, v.shape[0]), :] = v

    place_field(put, lambda at: own_f[at, :], 12, xg, yg, low)
    step = half_steps(fe, fh, factor)
    lane = lax.broadcasted_iota(jnp.int32, (1, W), 1)
    for n in range(STEPS):

        def use(b, olds, news):
            for i in range(6):
                inc[n, i, pl.ds(b, 8), :] = news[i] - olds[i]

        step(n, use)
        for s in range(2):
            x = cells[s, 0] - lax.axis_index("gx") * CX + HALO
            y = cells[s, 1] - lax.axis_index("gy") * CY + HALO
            for h in range(2):
                r = y - h * HY

                @pl.when((x >= 0) & (x < XR) & (r >= 0) & (r < TR))
                def _():
                    at = pl.ds(r * XR + x, 1)
                    pulse = jnp.where(lane == h * NZ + cells[s, 2], wave[s, n], 0.0).astype(F32)
                    fe[3 * s + 2, at, :] += pulse
                    inc[n, 3 * s + 2, at, :] += pulse


def adjoint(
    owners,
    slots,
    own_e,
    own_h,
    factor,
    inc,
    x_far,
    x_near,
    y_far,
    y_near,
    out,
    fe,
    fh,
    xg,
    yg,
    density,
    block,
):
    low = masks()[0]
    order_ghosts(x_near, x_far, y_near, y_far, 12, 12, xg, yg)

    def load(k, _):
        for ref, own, c in ((fe, own_e, 0), (fh, own_h, 3)):
            q = 6 * (k // 3) + k % 3 + c

            def put(r, v):
                ref[k, pl.ds(r, v.shape[0]), :] = v

            place_field(put, lambda at: own[k, at, :], q, xg, yg, low)
        return 0

    lax.fori_loop(0, 6, load, 0)
    step = half_steps(fe, fh, factor)
    for n in range(STEPS):

        def use(b, olds, news):
            terms = [news[i] * inc[STEPS - 1 - n, i, pl.ds(b, 8), :] for i in range(6)]
            total = ((terms[0] + terms[1]) + terms[2]) + ((terms[3] + terms[4]) + terms[5])
            if n > 0:
                total = total + density[pl.ds(b, 8), :]
            density[pl.ds(b, 8), :] = total

        step(n, use)

    for j in range(TJ // 2):
        for t in range(2):
            g = []
            for r in (2 * j + HALO, 2 * j + HALO + 1):
                at = pl.ds(r * XR + HALO + 8 * t, 8)
                g.append(density[at, :] * (factor[at, :] * (-1.0 / COURANT)))
            for tile, v in (
                (j, jnp.where(low, g[0], pltpu.roll(g[1], NZ, 1))),
                (j + TJ // 2, jnp.where(low, pltpu.roll(g[0], NZ, 1), g[1])),
            ):
                for h in range(2):
                    b = ((2 * t + h) * (TJ // 2) + tile // 2) * 8 + tile % 2
                    block[pl.ds(b, 4, stride=2), :] = v[4 * h : 4 * h + 4]
    out[...] = jnp.zeros_like(out)

    def send(i, _):
        o = owners[i // 16, i % 16]

        @pl.when(o >= 0)
        def _():
            c = pl.multiple_of(slots[i // 16, i % 16] * 4, 4)
            b = pl.multiple_of(i * 8, 8)
            out[2 * o, pl.ds(c, 4), :] = block[pl.ds(b, 4), :]
            out[2 * o + 1, pl.ds(c, 4), :] = block[pl.ds(b + 4, 4), :]

        return 0

    lax.fori_loop(0, 64, send, 0)


def place(rows, arrived, out, wide):
    def one(g, _):
        v = arrived[2 * g] + arrived[2 * g + 1]
        for c in range(4):
            r = pl.multiple_of(rows[0, g * 4 + c], 4)
            wide[pl.ds(r, 4), :] = v[c * 4 : c * 4 + 4]
        return 0

    lax.fori_loop(0, 16, one, 0)
    for i in range(8):
        for q in range(4):
            out[8 * i : 8 * i + 8, lanes(q)] = wide[pl.ds(32 * i + q, 8, stride=4), :]


FULL = pl.BlockSpec(memory_space=pltpu.VMEM)
SCALARS = pl.BlockSpec(memory_space=pltpu.SMEM)


def buf(*shape):
    return jax.ShapeDtypeStruct(shape, F32)


def call(kernel, n_scalars, n_arrays, outs, scratch=(), mib=8, us=2):
    return pl.pallas_call(
        kernel,
        in_specs=[SCALARS] * n_scalars + [FULL] * n_arrays,
        out_specs=[FULL] * len(outs),
        out_shape=list(outs),
        scratch_shapes=[pltpu.VMEM(shape, F32) for shape in scratch],
        compiler_params=pltpu.CompilerParams(vmem_limit_bytes=mib << 20),
        cost_estimate=pl.CostEstimate(
            flops=us * 1000000, bytes_accessed=us * 3000000, transcendentals=0
        ),
        name=kernel.__name__,
    )


RIM = (25, CX, 2 * W)


def call_pack_y():
    hbm = pl.BlockSpec(memory_space=pltpu.HBM)
    return pl.pallas_call(
        pack_y,
        in_specs=[hbm] * 3,
        out_specs=[FULL] * 2,
        out_shape=[buf(*RIM)] * 2,
        scratch_shapes=[pltpu.VMEM((2, CX, 2 * W), F32), pltpu.SemaphoreType.DMA((2, 5))],
        compiler_params=pltpu.CompilerParams(vmem_limit_bytes=62 << 20),
        name="pack_y",
    )


def call_pack_x(first, count):
    def kernel(*refs):
        pack_x(first, *refs)

    kernel.__name__ = "pack_x"
    return call(kernel, 0, 3 + (count == 13), [buf(count * TE * 4, W)] * 2, us=1)


FIELD = (6, ROWS, W)
SENT = (32, 16, W)


def call_forward():
    ghosts = [(2, 13 * TE * 4, W), (2, 13, CX, 2 * W)]
    return call(
        forward, 2, 7, [buf(STEPS, *FIELD), buf(ROWS, W)], [FIELD, FIELD, *ghosts], 12, 15
    )


def call_adjoint():
    ghosts = [(2, 12 * TE * 4, W), (2, 12, CX, 2 * W)]
    return call(
        adjoint,
        2,
        8,
        [buf(*SENT)],
        [FIELD, FIELD, *ghosts, (ROWS, W), (64 * 8, W)],
        12,
        15,
    )


def per_device(
    forward_state,
    adjoint_state,
    permittivity,
    waveform,
    source_cell,
    block_owner,
    block_slot,
    owner_rows,
):
    y_near, y_far = swapped(
        *call_pack_y()(forward_state, adjoint_state, permittivity), "gy"
    )
    own = [buf(6, TR * CX, W)] * 2
    forward_own = call(convert, 0, 2, [*own, buf(TR * CX, W)])(forward_state, permittivity)
    adjoint_own = call(convert, 0, 1, own)(adjoint_state)
    y_near, y_far, forward_own, adjoint_own = lax.optimization_barrier(
        (y_near, y_far, forward_own, adjoint_own)
    )
    fx_near, fx_far = swapped(
        *call_pack_x(0, 13)(forward_state, permittivity, y_far, y_near), "gx"
    )
    ax_near, ax_far = swapped(*call_pack_x(12, 12)(adjoint_state, y_far, y_near), "gx")
    inc, factor = call_forward()(
        source_cell, waveform, *forward_own, fx_far, fx_near, y_far, y_near
    )
    (outgoing,) = call_adjoint()(
        block_owner,
        block_slot,
        *adjoint_own,
        factor,
        inc,
        ax_far,
        ax_near,
        y_far,
        y_near,
    )
    outgoing, rows = lax.optimization_barrier((outgoing, owner_rows))
    arrived = lax.all_to_all(outgoing, ("gy", "src"), 0, 0, tiled=True)
    (placed,) = call(place, 1, 1, [buf(64, 512)], [(256, W)])(rows * 4, arrived)
    return placed


def solution(mesh):
    in_specs = (
        P("src", None, "gx", "gy"),
        P("src", None, "gx", "gy"),
        P("gx", "gy"),
        P("src", None),
        P("src", None),
        P("gx", "gy"),
        P("gx", "gy"),
        P(("gx", "gy"), None),
    )
    out_specs = P(("gx", "gy"), "src")
    return jax.shard_map(
        per_device, mesh=mesh, in_specs=in_specs, out_specs=out_specs, check_vma=False
    )
```

```python
import jax
import jax.numpy as jnp
from jax import lax
from jax.experimental import pallas as pl
from jax.experimental.pallas import tpu as pltpu
from jax.sharding import PartitionSpec as P

NZ = 64
STEPS = 4
HALO = 4
CX = 16
XR = CX + 2 * HALO
CY = 64
TJ = CY // 2
HY = CY // 2
TR = HY + 2 * HALO
TE = TJ + 4
ROWS = TR * XR
UNROLL = 6
W = 128
COURANT = 0.55
F32 = jnp.float32


def swapped(far, near, axis):
    count = lax.axis_size(axis)
    out = []
    for shard, first in ((near, 0), (far, 1)):
        pairs = [(i, i + 1) for i in range(first, count - 1, 2)]
        out.append(lax.ppermute(shard, axis, pairs + [(j, i) for i, j in pairs]))
    return out[0], out[1]


def lanes(tile):
    return pl.ds(tile * W, W)


def aligned(index, step):
    return index if isinstance(index, int) else pl.multiple_of(index, step)


def odd(axis):
    return lax.axis_index(axis) & 1


def pack_y(fwd, adj, eps, f_far, f_near, a_far, a_near, rim, sems):
    at = (1 - odd("gy")) * (TJ - 2)
    copies = []
    for i, (out_f, out_a, tile) in enumerate(((f_far, a_far, TJ - 2 - at), (f_near, a_near, at))):
        where = pl.ds(pl.multiple_of(tile * W, W), 2 * W)
        copies.append(pltpu.make_async_copy(eps.at[:, where], rim.at[i], sems.at[i, 4]))
        for n in range(4):
            state, out, src = (fwd, adj)[n // 2], (out_f, out_a)[n // 2], n % 2
            copies.append(
                pltpu.make_async_copy(
                    state.at[src, :, :, where], out.at[pl.ds(6 * src, 6)], sems.at[i, n]
                )
            )
    for copy in copies:
        copy.start()
    for i, out in enumerate((f_far, f_near)):
        copies[5 * i].wait()
        out[12] = COURANT / rim[i]
    for copy in copies[1:5] + copies[6:]:
        copy.wait()


def to_halves(own, put, low):
    for u in range(TR // 2):
        for x in (0, 8):
            a = own(x, u - 2) if u >= 2 else jnp.zeros((8, W), F32)
            b = own(x, u + 14) if u + 14 < TJ else jnp.zeros((8, W), F32)
            put(2 * u * CX + x, jnp.where(low, a, pltpu.roll(b, NZ, 1)))
            put((2 * u + 1) * CX + x, jnp.where(low, pltpu.roll(a, NZ, 1), b))


def convert(state, *rest):
    eps, e, h, factor = rest if len(rest) == 4 else (None, *rest, None)
    low = masks()[0]

    def one(k, _):
        for ref, c in ((e, 0), (h, 3)):

            def put(r, v):
                ref[k, pl.ds(r, 8), :] = v

            to_halves(lambda x, j: state[k // 3, k % 3 + c, x : x + 8, lanes(j)], put, low)
        return 0

    lax.fori_loop(0, 6, one, 0)
    if eps is not None:

        def put(r, v):
            factor[pl.ds(r, 8), :] = v

        to_halves(lambda x, j: COURANT / eps[x : x + 8, lanes(j)], put, low)


def pack_x(state, *rest):
    eps, y_far, y_near, far, near = rest if len(rest) == 5 else (None, *rest)

    def fill(lo, hi, dn, up):
        def put(k, get):
            for j in range(TE):
                row = aligned((k * TE + j) * 4, 4)
                for out, x in ((dn, 0), (up, CX - 4)):
                    if j < 2:
                        v = lo[k, x : x + 4, lanes(j)]
                    elif j >= TE - 2:
                        v = hi[k, x : x + 4, lanes(j - TE + 2)]
                    else:
                        v = get(x, lanes(j - 2))
                    out[pl.ds(row, 4), :] = v

        def one(k, _):
            put(k, lambda x, j: state[k // 6, k % 6, x : x + 4, j])
            return 0

        lax.fori_loop(0, 12, one, 0)
        if eps is not None:
            put(12, lambda x, j: COURANT / eps[x : x + 4, j])

    for px in range(2):
        for py in range(2):

            @pl.when((odd("gx") == px) & (odd("gy") == py))
            def _():
                ghosts = (y_far, y_near) if py == 0 else (y_near, y_far)
                outs = (far, near) if px == 0 else (near, far)
                fill(*ghosts, *outs)


def place_field(put, own, k, xg, yg, low):
    def from_x(side, j):
        return xg[side, pl.ds(aligned((k * TE + j + 2) * 4, 4), 4), :]

    for u in range(TR // 2):
        for side, x in ((0, 0), (1, HALO + CX)):
            a, b = from_x(side, u - 2), from_x(side, u - 2 + TJ // 2)
            put(2 * u * XR + x, jnp.where(low[:4], a, pltpu.roll(b, NZ, 1)))
            put((2 * u + 1) * XR + x, jnp.where(low[:4], pltpu.roll(a, NZ, 1), b))
        for x in (0, 8):
            for r in (2 * u, 2 * u + 1):
                v = own(pl.ds(r * CX + x, 8))
                if u < 2 or u >= TR // 2 - 2:
                    below = u < 2
                    g = yg[int(not below), k, pl.ds(x, 8), lanes(u if below else u - TR // 2 + 2)]
                    if below == bool(r % 2):
                        g = pltpu.roll(g, NZ, 1)
                    v = jnp.where(low, g, v) if below else jnp.where(low, v, g)
                put(r * XR + HALO + x, v)


def order_ghosts(x_near, x_far, y_near, y_far, xg, yg):
    px, py = odd("gx"), odd("gy")
    xg[1 - px] = x_near[...]
    xg[px] = x_far[...]
    yg[1 - py] = y_near[...]
    yg[py] = y_far[...]


def masks():
    lane = lax.broadcasted_iota(jnp.int32, (8, W), 1)
    return lane < NZ, (lane & (NZ - 1)) == 0, (lane & (NZ - 1)) == NZ - 1


def half_steps(fe, fh, factor):
    low, z_first, z_last = masks()
    row8 = lax.broadcasted_iota(jnp.int32, (8, W), 0)
    gx, gy = lax.axis_index("gx"), lax.axis_index("gy")
    at_x0, at_x1 = gx == 0, gx == lax.axis_size("gx") - 1
    at_y0, at_y1 = gy == 0, gy == lax.axis_size("gy") - 1
    coef_x = [
        jnp.where((row8 < 4) & at_x0, 0.0, COURANT).astype(F32),
        jnp.full((8, W), COURANT, F32),
        jnp.where((row8 >= 4) & at_x1, 0.0, COURANT).astype(F32),
    ]

    def up_z(v):
        return jnp.where(z_last, 0.0, pltpu.roll(v, W - 1, 1))

    def down_z(v):
        return jnp.where(z_first, 0.0, pltpu.roll(v, 1, 1))

    def magnetic(r):
        in_low = jnp.where((r < HALO) & at_y0, 0.0, 1.0).astype(F32)
        in_high = jnp.where((r >= HALO + HY) & at_y1, 0.0, 1.0).astype(F32)
        inside = jnp.where(low, in_low, in_high)
        for t in range(3):
            b = pl.multiple_of(r * XR + 8 * t, 8)
            c = coef_x[t] * inside
            for s in range(2):
                k = 3 * s
                ex = fe[k, pl.ds(b, 8), :]
                ey = fe[k + 1, pl.ds(b, 8), :]
                ez = fe[k + 2, pl.ds(b, 8), :]
                ex_y = fe[k, pl.ds(b + XR, 8), :]
                ez_y = fe[k + 2, pl.ds(b + XR, 8), :]
                ey_x = fe[k + 1, pl.ds(b + 1, 8), :]
                ez_x = fe[k + 2, pl.ds(b + 1, 8), :]
                hx = fh[k, pl.ds(b, 8), :] - c * ((ez_y - ez) - (up_z(ey) - ey))
                hy = fh[k + 1, pl.ds(b, 8), :] - c * ((up_z(ex) - ex) - (ez_x - ez))
                hz = fh[k + 2, pl.ds(b, 8), :] - c * ((ey_x - ey) - (ex_y - ex))
                fh[k, pl.ds(b, 8), :] = hx
                fh[k + 1, pl.ds(b, 8), :] = hy
                fh[k + 2, pl.ds(b, 8), :] = hz

    def electric(r, use):
        for t in range(3):
            b = pl.multiple_of(r * XR + 8 * t, 8)
            f = factor[pl.ds(b, 8), :]
            olds, news = [], []
            for s in range(2):
                k = 3 * s
                hx = fh[k, pl.ds(b, 8), :]
                hy = fh[k + 1, pl.ds(b, 8), :]
                hz = fh[k + 2, pl.ds(b, 8), :]
                hx_y = fh[k, pl.ds(b - XR, 8), :]
                hz_y = fh[k + 2, pl.ds(b - XR, 8), :]
                hy_x = fh[k + 1, pl.ds(b - 1, 8), :]
                hz_x = fh[k + 2, pl.ds(b - 1, 8), :]
                ex, ey, ez = (fe[k + c, pl.ds(b, 8), :] for c in range(3))
                nx = ex + f * ((hz - hz_y) - (hy - down_z(hy)))
                ny = ey + f * ((hx - down_z(hx)) - (hz - hz_x))
                nz = ez + f * ((hy - hy_x) - (hx - hx_y))
                fe[k, pl.ds(b, 8), :] = nx
                fe[k + 1, pl.ds(b, 8), :] = ny
                fe[k + 2, pl.ds(b, 8), :] = nz
                olds += [ex, ey, ez]
                news += [nx, ny, nz]
            use(b, olds, news)

    def over(first, last, one):
        def body(r, _):
            one(r)
            return 0

        lax.fori_loop(first, last, body, 0, unroll=UNROLL)

    def step(n, use):
        over(n, TR - 1 - n, magnetic)
        over(n + 1, TR - 1 - n, lambda r: electric(r, use))

    return step


def forward(
    cells,
    wave,
    own_e,
    own_h,
    own_f,
    x_far,
    x_near,
    y_far,
    y_near,
    inc,
    factor,
    fe,
    fh,
    xg,
    yg,
):
    low = masks()[0]
    order_ghosts(x_near, x_far, y_near, y_far, xg, yg)

    def load(k, _):
        for ref, own, c in ((fe, own_e, 0), (fh, own_h, 3)):
            q = 6 * (k // 3) + k % 3 + c

            def put(r, v):
                ref[k, pl.ds(r, v.shape[0]), :] = v

            place_field(put, lambda at: own[k, at, :], q, xg, yg, low)
        return 0

    lax.fori_loop(0, 6, load, 0)

    def put(r, v):
        factor[pl.ds(r, v.shape[0]), :] = v

    place_field(put, lambda at: own_f[at, :], 12, xg, yg, low)
    step = half_steps(fe, fh, factor)
    lane = lax.broadcasted_iota(jnp.int32, (1, W), 1)
    for n in range(STEPS):

        def use(b, olds, news):
            for i in range(6):
                inc[n, i, pl.ds(b, 8), :] = news[i] - olds[i]

        step(n, use)
        for s in range(2):
            x = cells[s, 0] - lax.axis_index("gx") * CX + HALO
            y = cells[s, 1] - lax.axis_index("gy") * CY + HALO
            for h in range(2):
                r = y - h * HY

                @pl.when((x >= 0) & (x < XR) & (r >= 0) & (r < TR))
                def _():
                    at = pl.ds(r * XR + x, 1)
                    pulse = jnp.where(lane == h * NZ + cells[s, 2], wave[s, n], 0.0).astype(F32)
                    fe[3 * s + 2, at, :] += pulse
                    inc[n, 3 * s + 2, at, :] += pulse


def adjoint(
    owners,
    slots,
    own_e,
    own_h,
    factor,
    inc,
    x_far,
    x_near,
    y_far,
    y_near,
    out,
    fe,
    fh,
    xg,
    yg,
    density,
    block,
):
    low = masks()[0]
    order_ghosts(x_near, x_far, y_near, y_far, xg, yg)

    def load(k, _):
        for ref, own, c in ((fe, own_e, 0), (fh, own_h, 3)):
            q = 6 * (k // 3) + k % 3 + c

            def put(r, v):
                ref[k, pl.ds(r, v.shape[0]), :] = v

            place_field(put, lambda at: own[k, at, :], q, xg, yg, low)
        return 0

    lax.fori_loop(0, 6, load, 0)
    step = half_steps(fe, fh, factor)
    for n in range(STEPS):

        def use(b, olds, news):
            terms = [news[i] * inc[STEPS - 1 - n, i, pl.ds(b, 8), :] for i in range(6)]
            total = ((terms[0] + terms[1]) + terms[2]) + ((terms[3] + terms[4]) + terms[5])
            if n > 0:
                total = total + density[pl.ds(b, 8), :]
            density[pl.ds(b, 8), :] = total

        step(n, use)

    for j in range(TJ // 2):
        for t in range(2):
            g = []
            for r in (2 * j + HALO, 2 * j + HALO + 1):
                at = pl.ds(r * XR + HALO + 8 * t, 8)
                g.append(density[at, :] * (factor[at, :] * (-1.0 / COURANT)))
            for tile, v in (
                (j, jnp.where(low, g[0], pltpu.roll(g[1], NZ, 1))),
                (j + TJ // 2, jnp.where(low, pltpu.roll(g[0], NZ, 1), g[1])),
            ):
                for h in range(2):
                    b = ((2 * t + h) * (TJ // 2) + tile // 2) * 8 + tile % 2
                    block[pl.ds(b, 4, stride=2), :] = v[4 * h : 4 * h + 4]
    out[...] = jnp.zeros_like(out)

    def send(i, _):
        o = owners[i // 16, i % 16]

        @pl.when(o >= 0)
        def _():
            c = pl.multiple_of(slots[i // 16, i % 16] * 4, 4)
            b = pl.multiple_of(i * 8, 8)
            out[2 * o, pl.ds(c, 4), :] = block[pl.ds(b, 4), :]
            out[2 * o + 1, pl.ds(c, 4), :] = block[pl.ds(b + 4, 4), :]

        return 0

    lax.fori_loop(0, 64, send, 0)


def place(rows, arrived, out, wide):
    def one(g, _):
        v = arrived[2 * g] + arrived[2 * g + 1]
        for c in range(4):
            r = pl.multiple_of(rows[0, g * 4 + c], 4)
            wide[pl.ds(r, 4), :] = v[c * 4 : c * 4 + 4]
        return 0

    lax.fori_loop(0, 16, one, 0)
    for i in range(8):
        for q in range(4):
            out[8 * i : 8 * i + 8, lanes(q)] = wide[pl.ds(32 * i + q, 8, stride=4), :]


FULL = pl.BlockSpec(memory_space=pltpu.VMEM)
SCALARS = pl.BlockSpec(memory_space=pltpu.SMEM)


def buf(*shape):
    return jax.ShapeDtypeStruct(shape, F32)


def call(kernel, n_scalars, n_arrays, outs, scratch=(), mib=8, us=2):
    return pl.pallas_call(
        kernel,
        in_specs=[SCALARS] * n_scalars + [FULL] * n_arrays,
        out_specs=[FULL] * len(outs),
        out_shape=list(outs),
        scratch_shapes=[pltpu.VMEM(shape, F32) for shape in scratch],
        compiler_params=pltpu.CompilerParams(vmem_limit_bytes=mib << 20),
        cost_estimate=pl.CostEstimate(
            flops=us * 1000000, bytes_accessed=us * 3000000, transcendentals=0
        ),
        name=kernel.__name__,
    )


RIM = (CX, 2 * W)


def call_pack_y():
    hbm = pl.BlockSpec(memory_space=pltpu.HBM)
    return pl.pallas_call(
        pack_y,
        in_specs=[hbm] * 3,
        out_specs=[FULL] * 4,
        out_shape=[buf(13, *RIM)] * 2 + [buf(12, *RIM)] * 2,
        scratch_shapes=[pltpu.VMEM((2, *RIM), F32), pltpu.SemaphoreType.DMA((2, 5))],
        compiler_params=pltpu.CompilerParams(vmem_limit_bytes=62 << 20),
        name="pack_y",
    )


def call_pack_x(count):
    return call(pack_x, 0, 3 + (count == 13), [buf(count * TE * 4, W)] * 2, us=1)


FIELD = (6, ROWS, W)
SENT = (32, 16, W)


def call_forward():
    ghosts = [(2, 13 * TE * 4, W), (2, 13, *RIM)]
    return call(
        forward, 2, 7, [buf(STEPS, *FIELD), buf(ROWS, W)], [FIELD, FIELD, *ghosts], 12, 15
    )


def call_adjoint():
    ghosts = [(2, 12 * TE * 4, W), (2, 12, *RIM)]
    return call(
        adjoint,
        2,
        8,
        [buf(*SENT)],
        [FIELD, FIELD, *ghosts, (ROWS, W), (64 * 8, W)],
        12,
        15,
    )


def per_device(
    forward_state,
    adjoint_state,
    permittivity,
    waveform,
    source_cell,
    block_owner,
    block_slot,
    owner_rows,
):
    rows_y = call_pack_y()(forward_state, adjoint_state, permittivity)
    fy_near, fy_far = swapped(*rows_y[:2], "gy")
    ay_near, ay_far = swapped(*rows_y[2:], "gy")
    own = [buf(6, TR * CX, W)] * 2
    forward_own = call(convert, 0, 2, [*own, buf(TR * CX, W)])(forward_state, permittivity)
    fy_near, fy_far, forward_own = lax.optimization_barrier((fy_near, fy_far, forward_own))
    fx_near, fx_far = swapped(
        *call_pack_x(13)(forward_state, permittivity, fy_far, fy_near), "gx"
    )
    ax_near, ax_far = swapped(*call_pack_x(12)(adjoint_state, ay_far, ay_near), "gx")
    adjoint_own = call(convert, 0, 1, own)(adjoint_state)
    fx_near, fx_far, adjoint_own = lax.optimization_barrier((fx_near, fx_far, adjoint_own))
    inc, factor = call_forward()(
        source_cell, waveform, *forward_own, fx_far, fx_near, fy_far, fy_near
    )
    (outgoing,) = call_adjoint()(
        block_owner,
        block_slot,
        *adjoint_own,
        factor,
        inc,
        ax_far,
        ax_near,
        ay_far,
        ay_near,
    )
    outgoing, rows = lax.optimization_barrier((outgoing, owner_rows))
    arrived = lax.all_to_all(outgoing, ("gy", "src"), 0, 0, tiled=True)
    (placed,) = call(place, 1, 1, [buf(64, 512)], [(256, W)])(rows * 4, arrived)
    return placed


def solution(mesh):
    in_specs = (
        P("src", None, "gx", "gy"),
        P("src", None, "gx", "gy"),
        P("gx", "gy"),
        P("src", None),
        P("src", None),
        P("gx", "gy"),
        P("gx", "gy"),
        P(("gx", "gy"), None),
    )
    out_specs = P(("gx", "gy"), "src")
    return jax.shard_map(
        per_device, mesh=mesh, in_specs=in_specs, out_specs=out_specs, check_vma=False
    )
```

```python
import jax
import jax.numpy as jnp
from jax import lax
from jax.experimental import pallas as pl
from jax.experimental.pallas import tpu as pltpu
from jax.sharding import PartitionSpec as P

NZ = 64
STEPS = 4
HALO = 4
CX = 16
XR = CX + 2 * HALO
CY = 64
TJ = CY // 2
HY = CY // 2
TR = HY + 2 * HALO
TE = TJ + 4
ROWS = TR * XR
UNROLL = 6
W = 128
COURANT = 0.55
F32 = jnp.float32


def swapped(far, near, axis):
    count = lax.axis_size(axis)
    out = []
    for shard, first in ((near, 0), (far, 1)):
        pairs = [(i, i + 1) for i in range(first, count - 1, 2)]
        out.append(lax.ppermute(shard, axis, pairs + [(j, i) for i, j in pairs]))
    return out[0], out[1]


def lanes(tile):
    return pl.ds(tile * W, W)


def aligned(index, step):
    return index if isinstance(index, int) else pl.multiple_of(index, step)


def odd(axis):
    return lax.axis_index(axis) & 1


def pack_y(fwd, adj, eps, f_far, f_near, a_far, a_near, rim, sems):
    at = (1 - odd("gy")) * (TJ - 2)
    copies = []
    for i, (out_f, out_a, tile) in enumerate(((f_far, a_far, TJ - 2 - at), (f_near, a_near, at))):
        where = pl.ds(pl.multiple_of(tile * W, W), 2 * W)
        copies.append(pltpu.make_async_copy(eps.at[:, where], rim.at[i], sems.at[i, 4]))
        for n in range(4):
            state, out, src = (fwd, adj)[n // 2], (out_f, out_a)[n // 2], n % 2
            copies.append(
                pltpu.make_async_copy(
                    state.at[src, :, :, where], out.at[pl.ds(6 * src, 6)], sems.at[i, n]
                )
            )
    for copy in copies:
        copy.start()
    for i, out in enumerate((f_far, f_near)):
        copies[5 * i].wait()
        out[12] = COURANT / rim[i]
    for copy in copies[1:5] + copies[6:]:
        copy.wait()


def to_halves(own, put, low):
    for u in range(TR // 2):
        for x in (0, 8):
            a = own(x, u - 2) if u >= 2 else jnp.zeros((8, W), F32)
            b = own(x, u + 14) if u + 14 < TJ else jnp.zeros((8, W), F32)
            put(2 * u * CX + x, jnp.where(low, a, pltpu.roll(b, NZ, 1)))
            put((2 * u + 1) * CX + x, jnp.where(low, pltpu.roll(a, NZ, 1), b))


def convert(state, *rest):
    eps, e, h, factor = rest if len(rest) == 4 else (None, *rest, None)
    low = masks()[0]

    def one(k, _):
        for ref, c in ((e, 0), (h, 3)):

            def put(r, v):
                ref[k, pl.ds(r, 8), :] = v

            to_halves(lambda x, j: state[k // 3, k % 3 + c, x : x + 8, lanes(j)], put, low)
        return 0

    lax.fori_loop(0, 6, one, 0)
    if eps is not None:

        def put(r, v):
            factor[pl.ds(r, 8), :] = v

        to_halves(lambda x, j: COURANT / eps[x : x + 8, lanes(j)], put, low)


def pack_x(state, *rest):
    eps, y_far, y_near, far, near = rest if len(rest) == 5 else (None, *rest)

    def fill(lo, hi, dn, up):
        def put(k, get):
            for j in range(TE):
                row = aligned((k * TE + j) * 4, 4)
                for out, x in ((dn, 0), (up, CX - 4)):
                    if j < 2:
                        v = lo[k, x : x + 4, lanes(j)]
                    elif j >= TE - 2:
                        v = hi[k, x : x + 4, lanes(j - TE + 2)]
                    else:
                        v = get(x, lanes(j - 2))
                    out[pl.ds(row, 4), :] = v

        def one(k, _):
            put(k, lambda x, j: state[k // 6, k % 6, x : x + 4, j])
            return 0

        lax.fori_loop(0, 12, one, 0)
        if eps is not None:
            put(12, lambda x, j: COURANT / eps[x : x + 4, j])

    for px in range(2):
        for py in range(2):

            @pl.when((odd("gx") == px) & (odd("gy") == py))
            def _():
                ghosts = (y_far, y_near) if py == 0 else (y_near, y_far)
                outs = (far, near) if px == 0 else (near, far)
                fill(*ghosts, *outs)


def place_field(put, own, k, xg, yg, low):
    def from_x(side, j):
        return xg[side, pl.ds(aligned((k * TE + j + 2) * 4, 4), 4), :]

    for u in range(TR // 2):
        for side, x in ((0, 0), (1, HALO + CX)):
            a, b = from_x(side, u - 2), from_x(side, u - 2 + TJ // 2)
            put(2 * u * XR + x, jnp.where(low[:4], a, pltpu.roll(b, NZ, 1)))
            put((2 * u + 1) * XR + x, jnp.where(low[:4], pltpu.roll(a, NZ, 1), b))
        for x in (0, 8):
            for r in (2 * u, 2 * u + 1):
                v = own(pl.ds(r * CX + x, 8))
                if u < 2 or u >= TR // 2 - 2:
                    below = u < 2
                    g = yg[int(not below), k, pl.ds(x, 8), lanes(u if below else u - TR // 2 + 2)]
                    if below == bool(r % 2):
                        g = pltpu.roll(g, NZ, 1)
                    v = jnp.where(low, g, v) if below else jnp.where(low, v, g)
                put(r * XR + HALO + x, v)


def order_ghosts(x_near, x_far, y_near, y_far, xg, yg):
    px, py = odd("gx"), odd("gy")
    xg[1 - px] = x_near[...]
    xg[px] = x_far[...]
    yg[1 - py] = y_near[...]
    yg[py] = y_far[...]


def masks():
    lane = lax.broadcasted_iota(jnp.int32, (8, W), 1)
    return lane < NZ, (lane & (NZ - 1)) == 0, (lane & (NZ - 1)) == NZ - 1


def half_steps(fe, fh, factor):
    low, z_first, z_last = masks()
    row8 = lax.broadcasted_iota(jnp.int32, (8, W), 0)
    gx, gy = lax.axis_index("gx"), lax.axis_index("gy")
    at_x0, at_x1 = gx == 0, gx == lax.axis_size("gx") - 1
    at_y0, at_y1 = gy == 0, gy == lax.axis_size("gy") - 1
    coef_x = [
        jnp.where((row8 < 4) & at_x0, 0.0, COURANT).astype(F32),
        jnp.full((8, W), COURANT, F32),
        jnp.where((row8 >= 4) & at_x1, 0.0, COURANT).astype(F32),
    ]

    def up_z(v):
        return jnp.where(z_last, 0.0, pltpu.roll(v, W - 1, 1))

    def down_z(v):
        return jnp.where(z_first, 0.0, pltpu.roll(v, 1, 1))

    def magnetic(r):
        in_low = jnp.where((r < HALO) & at_y0, 0.0, 1.0).astype(F32)
        in_high = jnp.where((r >= HALO + HY) & at_y1, 0.0, 1.0).astype(F32)
        inside = jnp.where(low, in_low, in_high)
        for t in range(3):
            b = pl.multiple_of(r * XR + 8 * t, 8)
            c = coef_x[t] * inside
            for s in range(2):
                k = 3 * s
                ex = fe[k, pl.ds(b, 8), :]
                ey = fe[k + 1, pl.ds(b, 8), :]
                ez = fe[k + 2, pl.ds(b, 8), :]
                ex_y = fe[k, pl.ds(b + XR, 8), :]
                ez_y = fe[k + 2, pl.ds(b + XR, 8), :]
                ey_x = fe[k + 1, pl.ds(b + 1, 8), :]
                ez_x = fe[k + 2, pl.ds(b + 1, 8), :]
                hx = fh[k, pl.ds(b, 8), :] - c * ((ez_y - ez) - (up_z(ey) - ey))
                hy = fh[k + 1, pl.ds(b, 8), :] - c * ((up_z(ex) - ex) - (ez_x - ez))
                hz = fh[k + 2, pl.ds(b, 8), :] - c * ((ey_x - ey) - (ex_y - ex))
                fh[k, pl.ds(b, 8), :] = hx
                fh[k + 1, pl.ds(b, 8), :] = hy
                fh[k + 2, pl.ds(b, 8), :] = hz

    def electric(r, use):
        for t in range(3):
            b = pl.multiple_of(r * XR + 8 * t, 8)
            f = factor[pl.ds(b, 8), :]
            olds, news = [], []
            for s in range(2):
                k = 3 * s
                hx = fh[k, pl.ds(b, 8), :]
                hy = fh[k + 1, pl.ds(b, 8), :]
                hz = fh[k + 2, pl.ds(b, 8), :]
                hx_y = fh[k, pl.ds(b - XR, 8), :]
                hz_y = fh[k + 2, pl.ds(b - XR, 8), :]
                hy_x = fh[k + 1, pl.ds(b - 1, 8), :]
                hz_x = fh[k + 2, pl.ds(b - 1, 8), :]
                ex, ey, ez = (fe[k + c, pl.ds(b, 8), :] for c in range(3))
                nx = ex + f * ((hz - hz_y) - (hy - down_z(hy)))
                ny = ey + f * ((hx - down_z(hx)) - (hz - hz_x))
                nz = ez + f * ((hy - hy_x) - (hx - hx_y))
                fe[k, pl.ds(b, 8), :] = nx
                fe[k + 1, pl.ds(b, 8), :] = ny
                fe[k + 2, pl.ds(b, 8), :] = nz
                olds += [ex, ey, ez]
                news += [nx, ny, nz]
            use(b, olds, news)

    def over(first, last, one):
        def body(r, _):
            one(r)
            return 0

        lax.fori_loop(first, last, body, 0, unroll=UNROLL)

    def step(n, use):
        over(n, TR - 1 - n, magnetic)
        over(n + 1, TR - 1 - n, lambda r: electric(r, use))

    return step


def forward(
    cells,
    wave,
    own_e,
    own_h,
    own_f,
    x_far,
    x_near,
    y_far,
    y_near,
    inc,
    factor,
    fe,
    fh,
    xg,
    yg,
):
    low = masks()[0]
    order_ghosts(x_near, x_far, y_near, y_far, xg, yg)

    def load(k, _):
        for ref, own, c in ((fe, own_e, 0), (fh, own_h, 3)):
            q = 6 * (k // 3) + k % 3 + c

            def put(r, v):
                ref[k, pl.ds(r, v.shape[0]), :] = v

            place_field(put, lambda at: own[k, at, :], q, xg, yg, low)
        return 0

    lax.fori_loop(0, 6, load, 0)

    def put(r, v):
        factor[pl.ds(r, v.shape[0]), :] = v

    place_field(put, lambda at: own_f[at, :], 12, xg, yg, low)
    step = half_steps(fe, fh, factor)
    lane = lax.broadcasted_iota(jnp.int32, (1, W), 1)
    for n in range(STEPS):

        def use(b, olds, news):
            for i in range(6):
                inc[n, i, pl.ds(b, 8), :] = news[i] - olds[i]

        step(n, use)
        for s in range(2):
            x = cells[s, 0] - lax.axis_index("gx") * CX + HALO
            y = cells[s, 1] - lax.axis_index("gy") * CY + HALO
            for h in range(2):
                r = y - h * HY

                @pl.when((x >= 0) & (x < XR) & (r >= 0) & (r < TR))
                def _():
                    at = pl.ds(r * XR + x, 1)
                    pulse = jnp.where(lane == h * NZ + cells[s, 2], wave[s, n], 0.0).astype(F32)
                    fe[3 * s + 2, at, :] += pulse
                    inc[n, 3 * s + 2, at, :] += pulse


def adjoint(
    owners,
    slots,
    own_e,
    own_h,
    factor,
    inc,
    x_far,
    x_near,
    y_far,
    y_near,
    keep,
    give,
    fe,
    fh,
    xg,
    yg,
    density,
    block,
):
    low = masks()[0]
    order_ghosts(x_near, x_far, y_near, y_far, xg, yg)

    def load(k, _):
        for ref, own, c in ((fe, own_e, 0), (fh, own_h, 3)):
            q = 6 * (k // 3) + k % 3 + c

            def put(r, v):
                ref[k, pl.ds(r, v.shape[0]), :] = v

            place_field(put, lambda at: own[k, at, :], q, xg, yg, low)
        return 0

    lax.fori_loop(0, 6, load, 0)
    step = half_steps(fe, fh, factor)
    for n in range(STEPS):

        def use(b, olds, news):
            terms = [news[i] * inc[STEPS - 1 - n, i, pl.ds(b, 8), :] for i in range(6)]
            total = ((terms[0] + terms[1]) + terms[2]) + ((terms[3] + terms[4]) + terms[5])
            if n > 0:
                total = total + density[pl.ds(b, 8), :]
            density[pl.ds(b, 8), :] = total

        step(n, use)

    for j in range(TJ // 2):
        for t in range(2):
            g = []
            for r in (2 * j + HALO, 2 * j + HALO + 1):
                at = pl.ds(r * XR + HALO + 8 * t, 8)
                g.append(density[at, :] * (factor[at, :] * (-1.0 / COURANT)))
            for tile, v in (
                (j, jnp.where(low, g[0], pltpu.roll(g[1], NZ, 1))),
                (j + TJ // 2, jnp.where(low, pltpu.roll(g[0], NZ, 1), g[1])),
            ):
                for h in range(2):
                    b = ((2 * t + h) * (TJ // 2) + tile // 2) * 8 + tile % 2
                    block[pl.ds(b, 4, stride=2), :] = v[4 * h : 4 * h + 4]
    keep[...] = jnp.zeros_like(keep)
    give[...] = jnp.zeros_like(give)
    mine = pl.multiple_of(lax.axis_index("src") * 4, 4)

    def send(i, _):
        o = owners[i // 16, i % 16]

        @pl.when(o >= 0)
        def _():
            c = pl.multiple_of(slots[i // 16, i % 16] * 4, 4)
            b = pl.multiple_of(i * 8, 8)
            keep[o, pl.ds(c, 4), :] = block[pl.ds(b + mine, 4), :]
            give[o, pl.ds(c, 4), :] = block[pl.ds(b + 4 - mine, 4), :]

        return 0

    lax.fori_loop(0, 64, send, 0)


def place(rows, arrived, out, wide):
    def one(g, _):
        v = arrived[g]
        for c in range(4):
            r = pl.multiple_of(rows[0, g * 4 + c], 4)
            wide[pl.ds(r, 4), :] = v[c * 4 : c * 4 + 4]
        return 0

    lax.fori_loop(0, 16, one, 0)
    for i in range(8):
        for q in range(4):
            out[8 * i : 8 * i + 8, lanes(q)] = wide[pl.ds(32 * i + q, 8, stride=4), :]


FULL = pl.BlockSpec(memory_space=pltpu.VMEM)
SCALARS = pl.BlockSpec(memory_space=pltpu.SMEM)


def buf(*shape):
    return jax.ShapeDtypeStruct(shape, F32)


def call(kernel, n_scalars, n_arrays, outs, scratch=(), mib=8, us=2):
    return pl.pallas_call(
        kernel,
        in_specs=[SCALARS] * n_scalars + [FULL] * n_arrays,
        out_specs=[FULL] * len(outs),
        out_shape=list(outs),
        scratch_shapes=[pltpu.VMEM(shape, F32) for shape in scratch],
        compiler_params=pltpu.CompilerParams(vmem_limit_bytes=mib << 20),
        cost_estimate=pl.CostEstimate(
            flops=us * 1000000, bytes_accessed=us * 3000000, transcendentals=0
        ),
        name=kernel.__name__,
    )


RIM = (CX, 2 * W)


def call_pack_y():
    hbm = pl.BlockSpec(memory_space=pltpu.HBM)
    return pl.pallas_call(
        pack_y,
        in_specs=[hbm] * 3,
        out_specs=[FULL] * 4,
        out_shape=[buf(13, *RIM)] * 2 + [buf(12, *RIM)] * 2,
        scratch_shapes=[pltpu.VMEM((2, *RIM), F32), pltpu.SemaphoreType.DMA((2, 5))],
        compiler_params=pltpu.CompilerParams(vmem_limit_bytes=62 << 20),
        name="pack_y",
    )


def call_pack_x(count):
    return call(pack_x, 0, 3 + (count == 13), [buf(count * TE * 4, W)] * 2, us=1)


FIELD = (6, ROWS, W)
SENT = (16, 16, W)


def call_forward():
    ghosts = [(2, 13 * TE * 4, W), (2, 13, *RIM)]
    return call(
        forward, 2, 7, [buf(STEPS, *FIELD), buf(ROWS, W)], [FIELD, FIELD, *ghosts], 12, 15
    )


def call_adjoint():
    ghosts = [(2, 12 * TE * 4, W), (2, 12, *RIM)]
    return call(
        adjoint,
        2,
        8,
        [buf(*SENT)] * 2,
        [FIELD, FIELD, *ghosts, (ROWS, W), (64 * 8, W)],
        12,
        15,
    )


def per_device(
    forward_state,
    adjoint_state,
    permittivity,
    waveform,
    source_cell,
    block_owner,
    block_slot,
    owner_rows,
):
    rows_y = call_pack_y()(forward_state, adjoint_state, permittivity)
    fy_near, fy_far = swapped(*rows_y[:2], "gy")
    ay_near, ay_far = swapped(*rows_y[2:], "gy")
    own = [buf(6, TR * CX, W)] * 2
    forward_own = call(convert, 0, 2, [*own, buf(TR * CX, W)])(forward_state, permittivity)
    fy_near, fy_far, forward_own = lax.optimization_barrier((fy_near, fy_far, forward_own))
    fx_near, fx_far = swapped(
        *call_pack_x(13)(forward_state, permittivity, fy_far, fy_near), "gx"
    )
    ax_near, ax_far = swapped(*call_pack_x(12)(adjoint_state, ay_far, ay_near), "gx")
    adjoint_own = call(convert, 0, 1, own)(adjoint_state)
    fx_near, fx_far, adjoint_own = lax.optimization_barrier((fx_near, fx_far, adjoint_own))
    inc, factor = call_forward()(
        source_cell, waveform, *forward_own, fx_far, fx_near, fy_far, fy_near
    )
    keep, give = call_adjoint()(
        block_owner,
        block_slot,
        *adjoint_own,
        factor,
        inc,
        ax_far,
        ax_near,
        ay_far,
        ay_near,
    )
    outgoing = keep + lax.ppermute(give, "src", [(0, 1), (1, 0)])
    outgoing, rows = lax.optimization_barrier((outgoing, owner_rows))
    arrived = lax.all_to_all(outgoing, "gy", 0, 0, tiled=True)
    (placed,) = call(place, 1, 1, [buf(64, 512)], [(256, W)])(rows * 4, arrived)
    return placed


def solution(mesh):
    in_specs = (
        P("src", None, "gx", "gy"),
        P("src", None, "gx", "gy"),
        P("gx", "gy"),
        P("src", None),
        P("src", None),
        P("gx", "gy"),
        P("gx", "gy"),
        P(("gx", "gy"), None),
    )
    out_specs = P(("gx", "gy"), "src")
    return jax.shard_map(
        per_device, mesh=mesh, in_specs=in_specs, out_specs=out_specs, check_vma=False
    )
```

```python
import jax
import jax.numpy as jnp
from jax import lax
from jax.experimental import pallas as pl
from jax.experimental.pallas import tpu as pltpu
from jax.sharding import PartitionSpec as P

NZ = 64
STEPS = 4
HALO = 4
CX = 16
XR = CX + 2 * HALO
CY = 64
TJ = CY // 2
HY = CY // 2
TR = HY + 2 * HALO
TE = TJ + 4
ROWS = TR * XR
LBY = CY // 4
LB = LBY * CX // 4
UNROLL = 8
W = 128
COURANT = 0.55
F32 = jnp.float32


def swapped(shard, axis, first):
    pairs = [(i, i + 1) for i in range(first, lax.axis_size(axis) - 1, 2)]
    return lax.ppermute(shard, axis, pairs + [(j, i) for i, j in pairs])


def lanes(tile):
    return pl.ds(tile * W, W)


def aligned(index, step):
    return index if isinstance(index, int) else pl.multiple_of(index, step)


def odd(axis):
    return lax.axis_index(axis) & 1


def pack_y(fwd, adj, eps, f_far, f_near, a_far, a_near, rim, sems):
    at = (1 - odd("gy")) * (TJ - 2)
    copies = []
    for i, (out_f, out_a, tile) in enumerate(((f_far, a_far, TJ - 2 - at), (f_near, a_near, at))):
        where = pl.ds(pl.multiple_of(tile * W, W), 2 * W)
        copies.append(pltpu.make_async_copy(eps.at[:, where], rim.at[i], sems.at[i, 4]))
        for n in range(4):
            state, out, src = (fwd, adj)[n // 2], (out_f, out_a)[n // 2], n % 2
            copies.append(
                pltpu.make_async_copy(
                    state.at[src, :, :, where], out.at[pl.ds(6 * src, 6)], sems.at[i, n]
                )
            )
    for copy in copies:
        copy.start()
    for i, out in enumerate((f_far, f_near)):
        copies[5 * i].wait()
        out[12] = COURANT / rim[i]
    for copy in copies[1:5] + copies[6:]:
        copy.wait()


def to_halves(own, put, low):
    for u in range(TR // 2):
        for x in (0, 8):
            a = own(x, u - 2) if u >= 2 else jnp.zeros((8, W), F32)
            b = own(x, u + 14) if u + 14 < TJ else jnp.zeros((8, W), F32)
            put(2 * u * CX + x, jnp.where(low, a, pltpu.roll(b, NZ, 1)))
            put((2 * u + 1) * CX + x, jnp.where(low, pltpu.roll(a, NZ, 1), b))


def convert(state, *rest):
    eps, e, h, factor = rest if len(rest) == 4 else (None, *rest, None)
    low = masks()[0]

    def one(k, _):
        for ref, c in ((e, 0), (h, 3)):

            def put(r, v):
                ref[k, pl.ds(r, 8), :] = v

            to_halves(lambda x, j: state[k // 3, k % 3 + c, x : x + 8, lanes(j)], put, low)
        return 0

    lax.fori_loop(0, 6, one, 0)
    if eps is not None:

        def put(r, v):
            factor[pl.ds(r, 8), :] = v

        to_halves(lambda x, j: COURANT / eps[x : x + 8, lanes(j)], put, low)


def pack_x(state, *rest):
    eps, y_far, y_near, far, near = rest if len(rest) == 5 else (None, *rest)

    def fill(lo, hi, dn, up):
        def put(k, get):
            for j in range(TE):
                row = aligned((k * TE + j) * 4, 4)
                for out, x in ((dn, 0), (up, CX - 4)):
                    if j < 2:
                        v = lo[k, x : x + 4, lanes(j)]
                    elif j >= TE - 2:
                        v = hi[k, x : x + 4, lanes(j - TE + 2)]
                    else:
                        v = get(x, lanes(j - 2))
                    out[pl.ds(row, 4), :] = v

        def one(k, _):
            put(k, lambda x, j: state[k // 6, k % 6, x : x + 4, j])
            return 0

        lax.fori_loop(0, 12, one, 0)
        if eps is not None:
            put(12, lambda x, j: COURANT / eps[x : x + 4, j])

    for px in range(2):
        for py in range(2):

            @pl.when((odd("gx") == px) & (odd("gy") == py))
            def _():
                ghosts = (y_far, y_near) if py == 0 else (y_near, y_far)
                outs = (far, near) if px == 0 else (near, far)
                fill(*ghosts, *outs)


def place_field(put, own, k, xg, yg, low):
    def from_x(side, j):
        return xg[side, pl.ds(aligned((k * TE + j + 2) * 4, 4), 4), :]

    for u in range(TR // 2):
        for side, x in ((0, 0), (1, HALO + CX)):
            a, b = from_x(side, u - 2), from_x(side, u - 2 + TJ // 2)
            put(2 * u * XR + x, jnp.where(low[:4], a, pltpu.roll(b, NZ, 1)))
            put((2 * u + 1) * XR + x, jnp.where(low[:4], pltpu.roll(a, NZ, 1), b))
        for x in (0, 8):
            for r in (2 * u, 2 * u + 1):
                v = own(pl.ds(r * CX + x, 8))
                if u < 2 or u >= TR // 2 - 2:
                    below = u < 2
                    g = yg[int(not below), k, pl.ds(x, 8), lanes(u if below else u - TR // 2 + 2)]
                    if below == bool(r % 2):
                        g = pltpu.roll(g, NZ, 1)
                    v = jnp.where(low, g, v) if below else jnp.where(low, v, g)
                put(r * XR + HALO + x, v)


def order_ghosts(x_near, x_far, y_near, y_far, xg, yg):
    px, py = odd("gx"), odd("gy")
    xg[1 - px] = x_near[...]
    xg[px] = x_far[...]
    yg[1 - py] = y_near[...]
    yg[py] = y_far[...]


def masks():
    lane = lax.broadcasted_iota(jnp.int32, (8, W), 1)
    return lane < NZ, (lane & (NZ - 1)) == 0, (lane & (NZ - 1)) == NZ - 1


def half_steps(fe, fh, factor):
    low, z_first, z_last = masks()
    row8 = lax.broadcasted_iota(jnp.int32, (8, W), 0)
    gx, gy = lax.axis_index("gx"), lax.axis_index("gy")
    at_x0, at_x1 = gx == 0, gx == lax.axis_size("gx") - 1
    at_y0, at_y1 = gy == 0, gy == lax.axis_size("gy") - 1
    coef_x = [
        jnp.where((row8 < 4) & at_x0, 0.0, COURANT).astype(F32),
        jnp.full((8, W), COURANT, F32),
        jnp.where((row8 >= 4) & at_x1, 0.0, COURANT).astype(F32),
    ]

    def up_z(v):
        return jnp.where(z_last, 0.0, pltpu.roll(v, W - 1, 1))

    def down_z(v):
        return jnp.where(z_first, 0.0, pltpu.roll(v, 1, 1))

    def magnetic(r):
        in_low = jnp.where((r < HALO) & at_y0, 0.0, 1.0).astype(F32)
        in_high = jnp.where((r >= HALO + HY) & at_y1, 0.0, 1.0).astype(F32)
        inside = jnp.where(low, in_low, in_high)
        for t in range(3):
            b = pl.multiple_of(r * XR + 8 * t, 8)
            c = coef_x[t] * inside
            for s in range(2):
                k = 3 * s
                ex = fe[k, pl.ds(b, 8), :]
                ey = fe[k + 1, pl.ds(b, 8), :]
                ez = fe[k + 2, pl.ds(b, 8), :]
                ex_y = fe[k, pl.ds(b + XR, 8), :]
                ez_y = fe[k + 2, pl.ds(b + XR, 8), :]
                ey_x = fe[k + 1, pl.ds(b + 1, 8), :]
                ez_x = fe[k + 2, pl.ds(b + 1, 8), :]
                hx = fh[k, pl.ds(b, 8), :] - c * ((ez_y - ez) - (up_z(ey) - ey))
                hy = fh[k + 1, pl.ds(b, 8), :] - c * ((up_z(ex) - ex) - (ez_x - ez))
                hz = fh[k + 2, pl.ds(b, 8), :] - c * ((ey_x - ey) - (ex_y - ex))
                fh[k, pl.ds(b, 8), :] = hx
                fh[k + 1, pl.ds(b, 8), :] = hy
                fh[k + 2, pl.ds(b, 8), :] = hz

    def electric(r, use):
        for t in range(3):
            b = pl.multiple_of(r * XR + 8 * t, 8)
            f = factor[pl.ds(b, 8), :]
            olds, news = [], []
            for s in range(2):
                k = 3 * s
                hx = fh[k, pl.ds(b, 8), :]
                hy = fh[k + 1, pl.ds(b, 8), :]
                hz = fh[k + 2, pl.ds(b, 8), :]
                hx_y = fh[k, pl.ds(b - XR, 8), :]
                hz_y = fh[k + 2, pl.ds(b - XR, 8), :]
                hy_x = fh[k + 1, pl.ds(b - 1, 8), :]
                hz_x = fh[k + 2, pl.ds(b - 1, 8), :]
                ex, ey, ez = (fe[k + c, pl.ds(b, 8), :] for c in range(3))
                nx = ex + f * ((hz - hz_y) - (hy - down_z(hy)))
                ny = ey + f * ((hx - down_z(hx)) - (hz - hz_x))
                nz = ez + f * ((hy - hy_x) - (hx - hx_y))
                fe[k, pl.ds(b, 8), :] = nx
                fe[k + 1, pl.ds(b, 8), :] = ny
                fe[k + 2, pl.ds(b, 8), :] = nz
                olds += [ex, ey, ez]
                news += [nx, ny, nz]
            use(b, olds, news)

    def over(first, last, one):
        def body(r, _):
            one(r)
            return 0

        lax.fori_loop(first, last, body, 0, unroll=UNROLL)

    def step(n, use):
        over(n, TR - 1 - n, magnetic)
        over(n + 1, TR - 1 - n, lambda r: electric(r, use))

    return step


def forward(
    cells,
    wave,
    own_e,
    own_h,
    own_f,
    x_far,
    x_near,
    y_far,
    y_near,
    inc,
    factor,
    fe,
    fh,
    xg,
    yg,
):
    low = masks()[0]
    order_ghosts(x_near, x_far, y_near, y_far, xg, yg)

    def load(k, _):
        for ref, own, c in ((fe, own_e, 0), (fh, own_h, 3)):
            q = 6 * (k // 3) + k % 3 + c

            def put(r, v):
                ref[k, pl.ds(r, v.shape[0]), :] = v

            place_field(put, lambda at: own[k, at, :], q, xg, yg, low)
        return 0

    lax.fori_loop(0, 6, load, 0)

    def put(r, v):
        factor[pl.ds(r, v.shape[0]), :] = v

    place_field(put, lambda at: own_f[at, :], 12, xg, yg, low)
    step = half_steps(fe, fh, factor)
    lane = lax.broadcasted_iota(jnp.int32, (1, W), 1)
    for n in range(STEPS):

        def use(b, olds, news):
            for i in range(6):
                inc[n, i, pl.ds(b, 8), :] = news[i] - olds[i]

        step(n, use)
        for s in range(2):
            x = cells[s, 0] - lax.axis_index("gx") * CX + HALO
            y = cells[s, 1] - lax.axis_index("gy") * CY + HALO
            for h in range(2):
                r = y - h * HY

                @pl.when((x >= 0) & (x < XR) & (r >= 0) & (r < TR))
                def _():
                    at = pl.ds(r * XR + x, 1)
                    pulse = jnp.where(lane == h * NZ + cells[s, 2], wave[s, n], 0.0).astype(F32)
                    fe[3 * s + 2, at, :] += pulse
                    inc[n, 3 * s + 2, at, :] += pulse


def adjoint(
    owners,
    slots,
    own_e,
    own_h,
    factor,
    inc,
    x_far,
    x_near,
    y_far,
    y_near,
    out,
    fe,
    fh,
    xg,
    yg,
    density,
    block,
    sent,
):
    low = masks()[0]
    order_ghosts(x_near, x_far, y_near, y_far, xg, yg)

    def load(k, _):
        for ref, own, c in ((fe, own_e, 0), (fh, own_h, 3)):
            q = 6 * (k // 3) + k % 3 + c

            def put(r, v):
                ref[k, pl.ds(r, v.shape[0]), :] = v

            place_field(put, lambda at: own[k, at, :], q, xg, yg, low)
        return 0

    lax.fori_loop(0, 6, load, 0)
    step = half_steps(fe, fh, factor)
    for n in range(STEPS):

        def use(b, olds, news):
            terms = [news[i] * inc[STEPS - 1 - n, i, pl.ds(b, 8), :] for i in range(6)]
            total = ((terms[0] + terms[1]) + terms[2]) + ((terms[3] + terms[4]) + terms[5])
            if n > 0:
                total = total + density[pl.ds(b, 8), :]
            density[pl.ds(b, 8), :] = total

        step(n, use)

    for j in range(TJ // 2):
        for t in range(2):
            g = []
            for r in (2 * j + HALO, 2 * j + HALO + 1):
                at = pl.ds(r * XR + HALO + 8 * t, 8)
                g.append(density[at, :] * (factor[at, :] * (-1.0 / COURANT)))
            for tile, v in (
                (j, jnp.where(low, g[0], pltpu.roll(g[1], NZ, 1))),
                (j + TJ // 2, jnp.where(low, pltpu.roll(g[0], NZ, 1), g[1])),
            ):
                for h in range(2):
                    b = ((2 * t + h) * (TJ // 2) + tile // 2) * 8 + tile % 2
                    block[pl.ds(b, 4, stride=2), :] = v[4 * h : 4 * h + 4]
    sent[...] = jnp.zeros_like(sent)
    for i in range(LB):
        o = owners[i // LBY, i % LBY]
        o0 = jnp.where(o < 0, 32, o)
        o1 = jnp.where(o < 0, 32, 16 + o)
        c = pl.multiple_of(jnp.maximum(slots[i // LBY, i % LBY], 0) * 4, 4)
        sent[o0, pl.ds(c, 4), :] = block[8 * i : 8 * i + 4, :]
        sent[o1, pl.ds(c, 4), :] = block[8 * i + 4 : 8 * i + 8, :]
    out[...] = sent[0:32]


def place(rows, arrived, out, wide):
    def one(g, _):
        v = arrived[g] + arrived[16 + g]
        for c in range(4):
            r = pl.multiple_of(rows[0, g * 4 + c] * 4, 4)
            wide[pl.ds(r, 4), :] = v[c * 4 : c * 4 + 4]
        return 0

    lax.fori_loop(0, 16, one, 0)
    for i in range(8):
        for q in range(4):
            out[8 * i : 8 * i + 8, lanes(q)] = wide[pl.ds(32 * i + q, 8, stride=4), :]


FULL = pl.BlockSpec(memory_space=pltpu.VMEM)
SCALARS = pl.BlockSpec(memory_space=pltpu.SMEM)


def buf(*shape):
    return jax.ShapeDtypeStruct(shape, F32)


def call(kernel, n_scalars, n_arrays, outs, scratch=(), mib=8, us=2):
    return pl.pallas_call(
        kernel,
        in_specs=[SCALARS] * n_scalars + [FULL] * n_arrays,
        out_specs=[FULL] * len(outs),
        out_shape=list(outs),
        scratch_shapes=[pltpu.VMEM(shape, F32) for shape in scratch],
        compiler_params=pltpu.CompilerParams(vmem_limit_bytes=mib << 20),
        cost_estimate=pl.CostEstimate(
            flops=us * 1000000, bytes_accessed=us * 3000000, transcendentals=0
        ),
        name=kernel.__name__,
    )


RIM = (CX, 2 * W)


def call_pack_y():
    hbm = pl.BlockSpec(memory_space=pltpu.HBM)
    return pl.pallas_call(
        pack_y,
        in_specs=[hbm] * 3,
        out_specs=[FULL] * 4,
        out_shape=[buf(13, *RIM)] * 2 + [buf(12, *RIM)] * 2,
        scratch_shapes=[pltpu.VMEM((2, *RIM), F32), pltpu.SemaphoreType.DMA((2, 5))],
        compiler_params=pltpu.CompilerParams(vmem_limit_bytes=62 << 20),
        name="pack_y",
    )


def call_pack_x(count):
    return call(pack_x, 0, 3 + (count == 13), [buf(count * TE * 4, W)] * 2, us=1)


FIELD = (6, ROWS, W)
SENT = (32, 16, W)


def call_forward():
    ghosts = [(2, 13 * TE * 4, W), (2, 13, *RIM)]
    return call(
        forward, 2, 7, [buf(STEPS, *FIELD), buf(ROWS, W)], [FIELD, FIELD, *ghosts], 12, 15
    )


def call_adjoint():
    ghosts = [(2, 12 * TE * 4, W), (2, 12, *RIM)]
    return call(
        adjoint,
        2,
        8,
        [buf(*SENT)],
        [FIELD, FIELD, *ghosts, (ROWS, W), (LB * 8, W), (33, 16, W)],
        12,
        15,
    )


def per_device(
    forward_state,
    adjoint_state,
    permittivity,
    waveform,
    source_cell,
    block_owner,
    block_slot,
    owner_rows,
):
    rows_y = call_pack_y()(forward_state, adjoint_state, permittivity)
    fy_far, fy_near = (swapped(rows_y[i], "gy", 1 - i) for i in range(2))
    ay_far, ay_near = (swapped(rows_y[2 + i], "gy", 1 - i) for i in range(2))
    own = [buf(6, TR * CX, W)] * 2
    adjoint_own = call(convert, 0, 1, own)(adjoint_state)
    fy_far, fy_near, adjoint_own = lax.optimization_barrier((fy_far, fy_near, adjoint_own))
    fx = call_pack_x(13)(forward_state, permittivity, fy_far, fy_near)
    fx_far, fx_near = (swapped(fx[i], "gx", 1 - i) for i in range(2))
    ax = call_pack_x(12)(adjoint_state, ay_far, ay_near)
    ax_near = swapped(ax[1], "gx", 0)
    forward_own = call(convert, 0, 2, [*own, buf(TR * CX, W)])(forward_state, permittivity)
    fx_far, ax_far, forward_own = lax.optimization_barrier((fx_far, ax[0], forward_own))
    ax_far = swapped(ax_far, "gx", 1)
    inc, factor = call_forward()(
        source_cell, waveform, *forward_own, fx_far, fx_near, fy_far, fy_near
    )
    (outgoing,) = call_adjoint()(
        block_owner,
        block_slot,
        *adjoint_own,
        factor,
        inc,
        ax_far,
        ax_near,
        ay_far,
        ay_near,
    )
    arrived = lax.all_to_all(outgoing, ("src", "gy"), 0, 0, tiled=True)
    (placed,) = call(place, 1, 1, [buf(64, 512)], [(256, W)])(owner_rows, arrived)
    return placed


def solution(mesh):
    in_specs = (
        P("src", None, "gx", "gy"),
        P("src", None, "gx", "gy"),
        P("gx", "gy"),
        P("src", None),
        P("src", None),
        P("gx", "gy"),
        P("gx", "gy"),
        P(("gx", "gy"), None),
    )
    out_specs = P(("gx", "gy"), "src")
    return jax.shard_map(
        per_device, mesh=mesh, in_specs=in_specs, out_specs=out_specs, check_vma=False
    )
```

```python
import jax
import jax.numpy as jnp
from jax import lax
from jax.experimental import pallas as pl
from jax.experimental.pallas import tpu as pltpu
from jax.sharding import PartitionSpec as P

NZ = 64
STEPS = 4
HALO = 4
CX = 16
XR = CX + 2 * HALO
CY = 64
TJ = CY // 2
HY = CY // 2
TR = HY + 2 * HALO
TE = TJ + 4
ROWS = TR * XR
LBY = CY // 4
LB = LBY * CX // 4
UNROLL = 16
W = 128
COURANT = 0.55
F32 = jnp.float32


def swapped(far, near, axis):
    count = lax.axis_size(axis)
    out = []
    for shard, first in ((near, 0), (far, 1)):
        pairs = [(i, i + 1) for i in range(first, count - 1, 2)]
        out.append(lax.ppermute(shard, axis, pairs + [(j, i) for i, j in pairs]))
    return out[0], out[1]


def lanes(tile):
    return pl.ds(tile * W, W)


def aligned(index, step):
    return index if isinstance(index, int) else pl.multiple_of(index, step)


def odd(axis):
    return lax.axis_index(axis) & 1


def pack_y(fwd, adj, eps, f_far, f_near, a_far, a_near, rim, sems):
    at = (1 - odd("gy")) * (TJ - 2)
    copies = []
    for i, (out_f, out_a, tile) in enumerate(((f_far, a_far, TJ - 2 - at), (f_near, a_near, at))):
        where = pl.ds(pl.multiple_of(tile * W, W), 2 * W)
        copies.append(pltpu.make_async_copy(eps.at[:, where], rim.at[i], sems.at[i, 4]))
        for n in range(4):
            state, out, src = (fwd, adj)[n // 2], (out_f, out_a)[n // 2], n % 2
            copies.append(
                pltpu.make_async_copy(
                    state.at[src, :, :, where], out.at[pl.ds(6 * src, 6)], sems.at[i, n]
                )
            )
    for copy in copies:
        copy.start()
    for i, out in enumerate((f_far, f_near)):
        copies[5 * i].wait()
        out[12] = COURANT / rim[i]
    for copy in copies[1:5] + copies[6:]:
        copy.wait()


def to_halves(own, put, low):
    for u in range(TR // 2):
        for x in (0, 8):
            a = own(x, u - 2) if u >= 2 else jnp.zeros((8, W), F32)
            b = own(x, u + 14) if u + 14 < TJ else jnp.zeros((8, W), F32)
            put(2 * u * CX + x, jnp.where(low, a, pltpu.roll(b, NZ, 1)))
            put((2 * u + 1) * CX + x, jnp.where(low, pltpu.roll(a, NZ, 1), b))


def convert(state, *rest):
    eps, e, h, factor = rest if len(rest) == 4 else (None, *rest, None)
    low = masks()[0]

    def one(k, _):
        for ref, c in ((e, 0), (h, 3)):

            def put(r, v):
                ref[k, pl.ds(r, 8), :] = v

            to_halves(lambda x, j: state[k // 3, k % 3 + c, x : x + 8, lanes(j)], put, low)
        return 0

    lax.fori_loop(0, 6, one, 0)
    if eps is not None:

        def put(r, v):
            factor[pl.ds(r, 8), :] = v

        to_halves(lambda x, j: COURANT / eps[x : x + 8, lanes(j)], put, low)


def pack_x(state, *rest):
    eps, y_far, y_near, far, near = rest if len(rest) == 5 else (None, *rest)

    def fill(lo, hi, dn, up):
        def put(k, get):
            for j in range(TE):
                row = aligned((k * TE + j) * 4, 4)
                for out, x in ((dn, 0), (up, CX - 4)):
                    if j < 2:
                        v = lo[k, x : x + 4, lanes(j)]
                    elif j >= TE - 2:
                        v = hi[k, x : x + 4, lanes(j - TE + 2)]
                    else:
                        v = get(x, lanes(j - 2))
                    out[pl.ds(row, 4), :] = v

        def one(k, _):
            put(k, lambda x, j: state[k // 6, k % 6, x : x + 4, j])
            return 0

        lax.fori_loop(0, 12, one, 0)
        if eps is not None:
            put(12, lambda x, j: COURANT / eps[x : x + 4, j])

    for px in range(2):
        for py in range(2):

            @pl.when((odd("gx") == px) & (odd("gy") == py))
            def _():
                ghosts = (y_far, y_near) if py == 0 else (y_near, y_far)
                outs = (far, near) if px == 0 else (near, far)
                fill(*ghosts, *outs)


def place_field(put, own, k, xg, yg, low):
    def from_x(side, j):
        return xg[side, pl.ds(aligned((k * TE + j + 2) * 4, 4), 4), :]

    for u in range(TR // 2):
        for side, x in ((0, 0), (1, HALO + CX)):
            a, b = from_x(side, u - 2), from_x(side, u - 2 + TJ // 2)
            put(2 * u * XR + x, jnp.where(low[:4], a, pltpu.roll(b, NZ, 1)))
            put((2 * u + 1) * XR + x, jnp.where(low[:4], pltpu.roll(a, NZ, 1), b))
        for x in (0, 8):
            for r in (2 * u, 2 * u + 1):
                v = own(pl.ds(r * CX + x, 8))
                if u < 2 or u >= TR // 2 - 2:
                    below = u < 2
                    g = yg[int(not below), k, pl.ds(x, 8), lanes(u if below else u - TR // 2 + 2)]
                    if below == bool(r % 2):
                        g = pltpu.roll(g, NZ, 1)
                    v = jnp.where(low, g, v) if below else jnp.where(low, v, g)
                put(r * XR + HALO + x, v)


def order_ghosts(x_near, x_far, y_near, y_far, xg, yg):
    px, py = odd("gx"), odd("gy")
    xg[1 - px] = x_near[...]
    xg[px] = x_far[...]
    yg[1 - py] = y_near[...]
    yg[py] = y_far[...]


def masks():
    lane = lax.broadcasted_iota(jnp.int32, (8, W), 1)
    return lane < NZ, (lane & (NZ - 1)) == 0, (lane & (NZ - 1)) == NZ - 1


def half_steps(fe, fh, factor):
    low, z_first, z_last = masks()
    row8 = lax.broadcasted_iota(jnp.int32, (8, W), 0)
    gx, gy = lax.axis_index("gx"), lax.axis_index("gy")
    at_x0, at_x1 = gx == 0, gx == lax.axis_size("gx") - 1
    at_y0, at_y1 = gy == 0, gy == lax.axis_size("gy") - 1
    coef_x = [
        jnp.where((row8 < 4) & at_x0, 0.0, COURANT).astype(F32),
        jnp.full((8, W), COURANT, F32),
        jnp.where((row8 >= 4) & at_x1, 0.0, COURANT).astype(F32),
    ]

    def up_z(v):
        return jnp.where(z_last, 0.0, pltpu.roll(v, W - 1, 1))

    def down_z(v):
        return jnp.where(z_first, 0.0, pltpu.roll(v, 1, 1))

    def magnetic(first, count, edge):
        for t in range(3):
            for s in range(2):
                k = 3 * s
                b = aligned(first * XR + 8 * t, 8)
                ex, ez = fe[k, pl.ds(b, 8), :], fe[k + 2, pl.ds(b, 8), :]
                for i in range(count):
                    b = aligned((first + i) * XR + 8 * t, 8)
                    c = coef_x[t]
                    if edge:
                        r = first + i
                        out = (low & at_y0) if r < HALO else (~low & at_y1)
                        c = jnp.where(out, 0.0, c)
                    ex_y, ez_y = fe[k, pl.ds(b + XR, 8), :], fe[k + 2, pl.ds(b + XR, 8), :]
                    ey = fe[k + 1, pl.ds(b, 8), :]
                    ey_x = fe[k + 1, pl.ds(b + 1, 8), :]
                    ez_x = fe[k + 2, pl.ds(b + 1, 8), :]
                    hx = fh[k, pl.ds(b, 8), :] - c * ((ez_y - ez) - (up_z(ey) - ey))
                    hy = fh[k + 1, pl.ds(b, 8), :] - c * ((up_z(ex) - ex) - (ez_x - ez))
                    hz = fh[k + 2, pl.ds(b, 8), :] - c * ((ey_x - ey) - (ex_y - ex))
                    fh[k, pl.ds(b, 8), :] = hx
                    fh[k + 1, pl.ds(b, 8), :] = hy
                    fh[k + 2, pl.ds(b, 8), :] = hz
                    ex, ez = ex_y, ez_y

    def electric(first, count, use):
        for t in range(3):
            for s in range(2):
                k = 3 * s
                b = aligned((first - 1) * XR + 8 * t, 8)
                hx_y, hz_y = fh[k, pl.ds(b, 8), :], fh[k + 2, pl.ds(b, 8), :]
                for i in range(count):
                    b = aligned((first + i) * XR + 8 * t, 8)
                    f = factor[pl.ds(b, 8), :]
                    hx, hy, hz = (fh[k + c, pl.ds(b, 8), :] for c in range(3))
                    hy_x = fh[k + 1, pl.ds(b - 1, 8), :]
                    hz_x = fh[k + 2, pl.ds(b - 1, 8), :]
                    ex, ey, ez = (fe[k + c, pl.ds(b, 8), :] for c in range(3))
                    nx = ex + f * ((hz - hz_y) - (hy - down_z(hy)))
                    ny = ey + f * ((hx - down_z(hx)) - (hz - hz_x))
                    nz = ez + f * ((hy - hy_x) - (hx - hx_y))
                    fe[k, pl.ds(b, 8), :] = nx
                    fe[k + 1, pl.ds(b, 8), :] = ny
                    fe[k + 2, pl.ds(b, 8), :] = nz
                    if use is not None:
                        use(s, b, (ex, ey, ez), (nx, ny, nz))
                    hx_y, hz_y = hx, hz

    def over(first, last, edge, inner):
        own = HALO + HY
        if first < HALO:
            edge(first, HALO - first)

        def body(i, _):
            inner(HALO + i * UNROLL, UNROLL)
            return 0

        lax.fori_loop(0, HY // UNROLL, body, 0)
        if last > own:
            edge(own, last - own)

    def step(n, use):
        over(
            n,
            TR - 1 - n,
            lambda r, m: magnetic(r, m, True),
            lambda r, m: magnetic(r, m, False),
        )
        over(
            n + 1,
            TR - 1 - n,
            lambda r, m: electric(r, m, None),
            lambda r, m: electric(r, m, use),
        )

    return step


def forward(
    cells,
    wave,
    own_e,
    own_h,
    own_f,
    x_far,
    x_near,
    y_far,
    y_near,
    inc,
    factor,
    fe,
    fh,
    xg,
    yg,
):
    low = masks()[0]
    order_ghosts(x_near, x_far, y_near, y_far, xg, yg)

    def load(k, _):
        for ref, own, c in ((fe, own_e, 0), (fh, own_h, 3)):
            q = 6 * (k // 3) + k % 3 + c

            def put(r, v):
                ref[k, pl.ds(r, v.shape[0]), :] = v

            place_field(put, lambda at: own[k, at, :], q, xg, yg, low)
        return 0

    lax.fori_loop(0, 6, load, 0)

    def put(r, v):
        factor[pl.ds(r, v.shape[0]), :] = v

    place_field(put, lambda at: own_f[at, :], 12, xg, yg, low)
    step = half_steps(fe, fh, factor)
    lane = lax.broadcasted_iota(jnp.int32, (1, W), 1)
    for n in range(STEPS):

        def use(s, b, olds, news):
            for c in range(3):
                inc[n, 3 * s + c, pl.ds(b, 8), :] = news[c] - olds[c]

        step(n, use)
        for s in range(2):
            x = cells[s, 0] - lax.axis_index("gx") * CX + HALO
            y = cells[s, 1] - lax.axis_index("gy") * CY + HALO
            for h in range(2):
                r = y - h * HY

                @pl.when((x >= 0) & (x < XR) & (r >= 0) & (r < TR))
                def _():
                    at = pl.ds(r * XR + x, 1)
                    pulse = jnp.where(lane == h * NZ + cells[s, 2], wave[s, n], 0.0).astype(F32)
                    fe[3 * s + 2, at, :] += pulse
                    inc[n, 3 * s + 2, at, :] += pulse


def adjoint(
    owners,
    slots,
    own_e,
    own_h,
    factor,
    inc,
    x_far,
    x_near,
    y_far,
    y_near,
    out,
    fe,
    fh,
    xg,
    yg,
    density,
    block,
    sent,
):
    low = masks()[0]
    order_ghosts(x_near, x_far, y_near, y_far, xg, yg)

    def load(k, _):
        for ref, own, c in ((fe, own_e, 0), (fh, own_h, 3)):
            q = 6 * (k // 3) + k % 3 + c

            def put(r, v):
                ref[k, pl.ds(r, v.shape[0]), :] = v

            place_field(put, lambda at: own[k, at, :], q, xg, yg, low)
        return 0

    lax.fori_loop(0, 6, load, 0)
    step = half_steps(fe, fh, factor)
    for n in range(STEPS):

        def use(s, b, olds, news):
            x, y, z = (
                news[c] * inc[STEPS - 1 - n, 3 * s + c, pl.ds(b, 8), :] for c in range(3)
            )
            total = (x + y) + z
            if n > 0:
                total = total + density[s, pl.ds(b, 8), :]
            density[s, pl.ds(b, 8), :] = total

        step(n, use)

    for j in range(TJ // 2):
        for t in range(2):
            g = []
            for r in (2 * j + HALO, 2 * j + HALO + 1):
                at = pl.ds(r * XR + HALO + 8 * t, 8)
                both = density[0, at, :] + density[1, at, :]
                g.append(both * (factor[at, :] * (-1.0 / COURANT)))
            for tile, v in (
                (j, jnp.where(low, g[0], pltpu.roll(g[1], NZ, 1))),
                (j + TJ // 2, jnp.where(low, pltpu.roll(g[0], NZ, 1), g[1])),
            ):
                for h in range(2):
                    b = ((2 * t + h) * (TJ // 2) + tile // 2) * 8 + tile % 2
                    block[pl.ds(b, 4, stride=2), :] = v[4 * h : 4 * h + 4]
    sent[...] = jnp.zeros_like(sent)
    for i in range(LB):
        o = owners[i // LBY, i % LBY]
        o0 = jnp.where(o < 0, 32, o)
        o1 = jnp.where(o < 0, 32, 16 + o)
        c = pl.multiple_of(jnp.maximum(slots[i // LBY, i % LBY], 0) * 4, 4)
        sent[o0, pl.ds(c, 4), :] = block[8 * i : 8 * i + 4, :]
        sent[o1, pl.ds(c, 4), :] = block[8 * i + 4 : 8 * i + 8, :]
    out[...] = sent[0:32]


def place(rows, arrived, out, wide):
    def one(g, _):
        v = arrived[g] + arrived[16 + g]
        for c in range(4):
            r = pl.multiple_of(rows[0, g * 4 + c] * 4, 4)
            wide[pl.ds(r, 4), :] = v[c * 4 : c * 4 + 4]
        return 0

    lax.fori_loop(0, 16, one, 0)
    for i in range(8):
        for q in range(4):
            out[8 * i : 8 * i + 8, lanes(q)] = wide[pl.ds(32 * i + q, 8, stride=4), :]


FULL = pl.BlockSpec(memory_space=pltpu.VMEM)
SCALARS = pl.BlockSpec(memory_space=pltpu.SMEM)


def buf(*shape):
    return jax.ShapeDtypeStruct(shape, F32)


def call(kernel, n_scalars, n_arrays, outs, scratch=(), mib=8, us=2):
    return pl.pallas_call(
        kernel,
        in_specs=[SCALARS] * n_scalars + [FULL] * n_arrays,
        out_specs=[FULL] * len(outs),
        out_shape=list(outs),
        scratch_shapes=[pltpu.VMEM(shape, F32) for shape in scratch],
        compiler_params=pltpu.CompilerParams(vmem_limit_bytes=mib << 20),
        cost_estimate=pl.CostEstimate(
            flops=us * 1000000, bytes_accessed=us * 3000000, transcendentals=0
        ),
        name=kernel.__name__,
    )


RIM = (CX, 2 * W)


def call_pack_y():
    hbm = pl.BlockSpec(memory_space=pltpu.HBM)
    return pl.pallas_call(
        pack_y,
        in_specs=[hbm] * 3,
        out_specs=[FULL] * 4,
        out_shape=[buf(13, *RIM)] * 2 + [buf(12, *RIM)] * 2,
        scratch_shapes=[pltpu.VMEM((2, *RIM), F32), pltpu.SemaphoreType.DMA((2, 5))],
        compiler_params=pltpu.CompilerParams(vmem_limit_bytes=62 << 20),
        name="pack_y",
    )


def call_pack_x(count):
    return call(pack_x, 0, 3 + (count == 13), [buf(count * TE * 4, W)] * 2, us=1)


FIELD = (6, ROWS, W)
SENT = (32, 16, W)


def call_forward():
    ghosts = [(2, 13 * TE * 4, W), (2, 13, *RIM)]
    return call(
        forward, 2, 7, [buf(STEPS, *FIELD), buf(ROWS, W)], [FIELD, FIELD, *ghosts], 12, 15
    )


def call_adjoint():
    ghosts = [(2, 12 * TE * 4, W), (2, 12, *RIM)]
    return call(
        adjoint,
        2,
        8,
        [buf(*SENT)],
        [FIELD, FIELD, *ghosts, (2, ROWS, W), (LB * 8, W), (33, 16, W)],
        12,
        15,
    )


def per_device(
    forward_state,
    adjoint_state,
    permittivity,
    waveform,
    source_cell,
    block_owner,
    block_slot,
    owner_rows,
):
    rows_y = call_pack_y()(forward_state, adjoint_state, permittivity)
    fy_near, fy_far = swapped(*rows_y[:2], "gy")
    ay_near, ay_far = swapped(*rows_y[2:], "gy")
    own = [buf(6, TR * CX, W)] * 2
    forward_own = call(convert, 0, 2, [*own, buf(TR * CX, W)])(forward_state, permittivity)
    fy_near, fy_far, forward_own = lax.optimization_barrier((fy_near, fy_far, forward_own))
    fx_near, fx_far = swapped(
        *call_pack_x(13)(forward_state, permittivity, fy_far, fy_near), "gx"
    )
    ax_near, ax_far = swapped(*call_pack_x(12)(adjoint_state, ay_far, ay_near), "gx")
    adjoint_own = call(convert, 0, 1, own)(adjoint_state)
    fx_near, fx_far, adjoint_own = lax.optimization_barrier((fx_near, fx_far, adjoint_own))
    inc, factor = call_forward()(
        source_cell, waveform, *forward_own, fx_far, fx_near, fy_far, fy_near
    )
    (outgoing,) = call_adjoint()(
        block_owner,
        block_slot,
        *adjoint_own,
        factor,
        inc,
        ax_far,
        ax_near,
        ay_far,
        ay_near,
    )
    arrived = lax.all_to_all(outgoing, ("src", "gy"), 0, 0, tiled=True)
    (placed,) = call(place, 1, 1, [buf(64, 512)], [(256, W)])(owner_rows, arrived)
    return placed


def solution(mesh):
    in_specs = (
        P("src", None, "gx", "gy"),
        P("src", None, "gx", "gy"),
        P("gx", "gy"),
        P("src", None),
        P("src", None),
        P("gx", "gy"),
        P("gx", "gy"),
        P(("gx", "gy"), None),
    )
    out_specs = P(("gx", "gy"), "src")
    return jax.shard_map(
        per_device, mesh=mesh, in_specs=in_specs, out_specs=out_specs, check_vma=False
    )
```

```python
import jax
import jax.numpy as jnp
from jax import lax
from jax.experimental import pallas as pl
from jax.experimental.pallas import tpu as pltpu
from jax.sharding import PartitionSpec as P

NZ = 64
STEPS = 4
HALO = 4
CX = 16
XR = CX + 2 * HALO
CY = 64
TJ = CY // 2
HY = CY // 2
TR = HY + 2 * HALO
TE = TJ + 4
ROWS = TR * XR
LBY = CY // 4
LB = LBY * CX // 4
UNROLL = 16
W = 128
COURANT = 0.55
F32 = jnp.float32


def swapped(far, near, axis):
    count = lax.axis_size(axis)
    out = []
    for shard, first in ((near, 0), (far, 1)):
        pairs = [(i, i + 1) for i in range(first, count - 1, 2)]
        out.append(lax.ppermute(shard, axis, pairs + [(j, i) for i, j in pairs]))
    return out[0], out[1]


def lanes(tile):
    return pl.ds(tile * W, W)


def aligned(index, step):
    return index if isinstance(index, int) else pl.multiple_of(index, step)


def odd(axis):
    return lax.axis_index(axis) & 1


def pack_y(fwd, adj, eps, f_far, f_near, a_far, a_near, rim, sems):
    at = (1 - odd("gy")) * (TJ - 2)
    copies = []
    for i, (out_f, out_a, tile) in enumerate(((f_far, a_far, TJ - 2 - at), (f_near, a_near, at))):
        where = pl.ds(pl.multiple_of(tile * W, W), 2 * W)
        copies.append(pltpu.make_async_copy(eps.at[:, where], rim.at[i], sems.at[i, 4]))
        for n in range(4):
            state, out, src = (fwd, adj)[n // 2], (out_f, out_a)[n // 2], n % 2
            copies.append(
                pltpu.make_async_copy(
                    state.at[src, :, :, where], out.at[pl.ds(6 * src, 6)], sems.at[i, n]
                )
            )
    for copy in copies:
        copy.start()
    for i, out in enumerate((f_far, f_near)):
        copies[5 * i].wait()
        out[12] = COURANT / rim[i]
    for copy in copies[1:5] + copies[6:]:
        copy.wait()


def to_halves(own, put, low):
    for u in range(TR // 2):
        for x in (0, 8):
            a = own(x, u - 2) if u >= 2 else jnp.zeros((8, W), F32)
            b = own(x, u + 14) if u + 14 < TJ else jnp.zeros((8, W), F32)
            put(2 * u * CX + x, jnp.where(low, a, pltpu.roll(b, NZ, 1)))
            put((2 * u + 1) * CX + x, jnp.where(low, pltpu.roll(a, NZ, 1), b))


def convert(state, *rest):
    eps, e, h, factor = rest if len(rest) == 4 else (None, *rest, None)
    low = masks()[0]

    def one(k, _):
        for ref, c in ((e, 0), (h, 3)):

            def put(r, v):
                ref[k, pl.ds(r, 8), :] = v

            to_halves(lambda x, j: state[k // 3, k % 3 + c, x : x + 8, lanes(j)], put, low)
        return 0

    lax.fori_loop(0, 6, one, 0)
    if eps is not None:

        def put(r, v):
            factor[pl.ds(r, 8), :] = v

        to_halves(lambda x, j: COURANT / eps[x : x + 8, lanes(j)], put, low)


def pack_x(state, *rest):
    eps, y_far, y_near, far, near = rest if len(rest) == 5 else (None, *rest)

    def fill(lo, hi, dn, up):
        def put(k, get):
            for j in range(TE):
                row = aligned((k * TE + j) * 4, 4)
                for out, x in ((dn, 0), (up, CX - 4)):
                    if j < 2:
                        v = lo[k, x : x + 4, lanes(j)]
                    elif j >= TE - 2:
                        v = hi[k, x : x + 4, lanes(j - TE + 2)]
                    else:
                        v = get(x, lanes(j - 2))
                    out[pl.ds(row, 4), :] = v

        def one(k, _):
            put(k, lambda x, j: state[k // 6, k % 6, x : x + 4, j])
            return 0

        lax.fori_loop(0, 12, one, 0)
        if eps is not None:
            put(12, lambda x, j: COURANT / eps[x : x + 4, j])

    for px in range(2):
        for py in range(2):

            @pl.when((odd("gx") == px) & (odd("gy") == py))
            def _():
                ghosts = (y_far, y_near) if py == 0 else (y_near, y_far)
                outs = (far, near) if px == 0 else (near, far)
                fill(*ghosts, *outs)


def place_field(put, own, k, xg, yg, low):
    def from_x(side, j):
        return xg[side, pl.ds(aligned((k * TE + j + 2) * 4, 4), 4), :]

    for u in range(TR // 2):
        for side, x in ((0, 0), (1, HALO + CX)):
            a, b = from_x(side, u - 2), from_x(side, u - 2 + TJ // 2)
            put(2 * u * XR + x, jnp.where(low[:4], a, pltpu.roll(b, NZ, 1)))
            put((2 * u + 1) * XR + x, jnp.where(low[:4], pltpu.roll(a, NZ, 1), b))
        for x in (0, 8):
            for r in (2 * u, 2 * u + 1):
                v = own(pl.ds(r * CX + x, 8))
                if u < 2 or u >= TR // 2 - 2:
                    below = u < 2
                    g = yg[int(not below), k, pl.ds(x, 8), lanes(u if below else u - TR // 2 + 2)]
                    if below == bool(r % 2):
                        g = pltpu.roll(g, NZ, 1)
                    v = jnp.where(low, g, v) if below else jnp.where(low, v, g)
                put(r * XR + HALO + x, v)


def order_ghosts(x_near, x_far, y_near, y_far, xg, yg):
    px, py = odd("gx"), odd("gy")
    xg[1 - px] = x_near[...]
    xg[px] = x_far[...]
    yg[1 - py] = y_near[...]
    yg[py] = y_far[...]


def masks():
    lane = lax.broadcasted_iota(jnp.int32, (8, W), 1)
    return lane < NZ, (lane & (NZ - 1)) == 0, (lane & (NZ - 1)) == NZ - 1


def half_steps(fe, fh, factor):
    low, z_first, z_last = masks()
    row8 = lax.broadcasted_iota(jnp.int32, (8, W), 0)
    gx, gy = lax.axis_index("gx"), lax.axis_index("gy")
    at_x0, at_x1 = gx == 0, gx == lax.axis_size("gx") - 1
    at_y0, at_y1 = gy == 0, gy == lax.axis_size("gy") - 1
    coef_x = [
        jnp.where((row8 < 4) & at_x0, 0.0, COURANT).astype(F32),
        jnp.full((8, W), COURANT, F32),
        jnp.where((row8 >= 4) & at_x1, 0.0, COURANT).astype(F32),
    ]

    def up_z(v):
        return jnp.where(z_last, 0.0, pltpu.roll(v, W - 1, 1))

    def down_z(v):
        return jnp.where(z_first, 0.0, pltpu.roll(v, 1, 1))

    def magnetic(first, count, edge):
        for t in range(3):
            for s in range(2):
                k = 3 * s
                b = aligned(first * XR + 8 * t, 8)
                ex, ez = fe[k, pl.ds(b, 8), :], fe[k + 2, pl.ds(b, 8), :]
                for i in range(count):
                    b = aligned((first + i) * XR + 8 * t, 8)
                    c = coef_x[t]
                    if edge:
                        r = first + i
                        out = (low & at_y0) if r < HALO else (~low & at_y1)
                        c = jnp.where(out, 0.0, c)
                    ex_y, ez_y = fe[k, pl.ds(b + XR, 8), :], fe[k + 2, pl.ds(b + XR, 8), :]
                    ey = fe[k + 1, pl.ds(b, 8), :]
                    ey_x = fe[k + 1, pl.ds(b + 1, 8), :]
                    ez_x = fe[k + 2, pl.ds(b + 1, 8), :]
                    hx = fh[k, pl.ds(b, 8), :] - c * ((ez_y - ez) - (up_z(ey) - ey))
                    hy = fh[k + 1, pl.ds(b, 8), :] - c * ((up_z(ex) - ex) - (ez_x - ez))
                    hz = fh[k + 2, pl.ds(b, 8), :] - c * ((ey_x - ey) - (ex_y - ex))
                    fh[k, pl.ds(b, 8), :] = hx
                    fh[k + 1, pl.ds(b, 8), :] = hy
                    fh[k + 2, pl.ds(b, 8), :] = hz
                    ex, ez = ex_y, ez_y

    def electric(first, count, use):
        for t in range(3):
            for s in range(2):
                k = 3 * s
                b = aligned((first - 1) * XR + 8 * t, 8)
                hx_y, hz_y = fh[k, pl.ds(b, 8), :], fh[k + 2, pl.ds(b, 8), :]
                for i in range(count):
                    b = aligned((first + i) * XR + 8 * t, 8)
                    f = factor[pl.ds(b, 8), :]
                    hx, hy, hz = (fh[k + c, pl.ds(b, 8), :] for c in range(3))
                    hy_x = fh[k + 1, pl.ds(b - 1, 8), :]
                    hz_x = fh[k + 2, pl.ds(b - 1, 8), :]
                    ex, ey, ez = (fe[k + c, pl.ds(b, 8), :] for c in range(3))
                    nx = ex + f * ((hz - hz_y) - (hy - down_z(hy)))
                    ny = ey + f * ((hx - down_z(hx)) - (hz - hz_x))
                    nz = ez + f * ((hy - hy_x) - (hx - hx_y))
                    fe[k, pl.ds(b, 8), :] = nx
                    fe[k + 1, pl.ds(b, 8), :] = ny
                    fe[k + 2, pl.ds(b, 8), :] = nz
                    if use is not None:
                        use(s, b, (ex, ey, ez), (nx, ny, nz))
                    hx_y, hz_y = hx, hz

    def over(first, last, edge, inner):
        own = HALO + HY
        if first < HALO:
            edge(first, HALO - first)

        def body(i, _):
            inner(HALO + i * UNROLL, UNROLL)
            return 0

        lax.fori_loop(0, HY // UNROLL, body, 0)
        if last > own:
            edge(own, last - own)

    def step(n, use):
        over(
            n,
            TR - 1 - n,
            lambda r, m: magnetic(r, m, True),
            lambda r, m: magnetic(r, m, False),
        )
        over(
            n + 1,
            TR - 1 - n,
            lambda r, m: electric(r, m, None),
            lambda r, m: electric(r, m, use),
        )

    return step


def forward(
    cells,
    wave,
    own_e,
    own_h,
    own_f,
    x_far,
    x_near,
    y_far,
    y_near,
    inc,
    factor,
    fe,
    fh,
    xg,
    yg,
):
    low = masks()[0]
    order_ghosts(x_near, x_far, y_near, y_far, xg, yg)

    def load(k, _):
        for ref, own, c in ((fe, own_e, 0), (fh, own_h, 3)):
            q = 6 * (k // 3) + k % 3 + c

            def put(r, v):
                ref[k, pl.ds(r, v.shape[0]), :] = v

            place_field(put, lambda at: own[k, at, :], q, xg, yg, low)
        return 0

    lax.fori_loop(0, 6, load, 0)

    def put(r, v):
        factor[pl.ds(r, v.shape[0]), :] = v

    place_field(put, lambda at: own_f[at, :], 12, xg, yg, low)
    step = half_steps(fe, fh, factor)
    lane = lax.broadcasted_iota(jnp.int32, (1, W), 1)
    for n in range(STEPS):

        def use(s, b, olds, news):
            for c in range(3):
                inc[n, 3 * s + c, pl.ds(b, 8), :] = news[c] - olds[c]

        step(n, use)
        for s in range(2):
            x = cells[s, 0] - lax.axis_index("gx") * CX + HALO
            y = cells[s, 1] - lax.axis_index("gy") * CY + HALO
            for h in range(2):
                r = y - h * HY

                @pl.when((x >= 0) & (x < XR) & (r >= 0) & (r < TR))
                def _():
                    at = pl.ds(r * XR + x, 1)
                    pulse = jnp.where(lane == h * NZ + cells[s, 2], wave[s, n], 0.0).astype(F32)
                    fe[3 * s + 2, at, :] += pulse
                    inc[n, 3 * s + 2, at, :] += pulse


def adjoint(
    owners,
    slots,
    own_e,
    own_h,
    factor,
    inc,
    x_far,
    x_near,
    y_far,
    y_near,
    out,
    fe,
    fh,
    xg,
    yg,
    density,
    block,
    sent,
):
    low = masks()[0]
    order_ghosts(x_near, x_far, y_near, y_far, xg, yg)

    def load(k, _):
        for ref, own, c in ((fe, own_e, 0), (fh, own_h, 3)):
            q = 6 * (k // 3) + k % 3 + c

            def put(r, v):
                ref[k, pl.ds(r, v.shape[0]), :] = v

            place_field(put, lambda at: own[k, at, :], q, xg, yg, low)
        return 0

    lax.fori_loop(0, 6, load, 0)
    step = half_steps(fe, fh, factor)
    for n in range(STEPS):

        def use(s, b, olds, news):
            x, y, z = (
                news[c] * inc[STEPS - 1 - n, 3 * s + c, pl.ds(b, 8), :] for c in range(3)
            )
            total = (x + y) + z
            if n > 0:
                total = total + density[s, pl.ds(b, 8), :]
            density[s, pl.ds(b, 8), :] = total

        step(n, use)

    for j in range(TJ // 2):
        for t in range(2):
            g = []
            for r in (2 * j + HALO, 2 * j + HALO + 1):
                at = pl.ds(r * XR + HALO + 8 * t, 8)
                both = density[0, at, :] + density[1, at, :]
                g.append(both * (factor[at, :] * (-1.0 / COURANT)))
            for tile, v in (
                (j, jnp.where(low, g[0], pltpu.roll(g[1], NZ, 1))),
                (j + TJ // 2, jnp.where(low, pltpu.roll(g[0], NZ, 1), g[1])),
            ):
                for h in range(2):
                    b = ((2 * t + h) * (TJ // 2) + tile // 2) * 8 + tile % 2
                    block[pl.ds(b, 4, stride=2), :] = v[4 * h : 4 * h + 4]
    sent[...] = jnp.zeros_like(sent)
    for i in range(LB):
        o = owners[i // LBY, i % LBY]
        o0 = jnp.where(o < 0, 32, o)
        o1 = jnp.where(o < 0, 32, 16 + o)
        c = pl.multiple_of(jnp.maximum(slots[i // LBY, i % LBY], 0) * 4, 4)
        sent[o0, pl.ds(c, 4), :] = block[8 * i : 8 * i + 4, :]
        sent[o1, pl.ds(c, 4), :] = block[8 * i + 4 : 8 * i + 8, :]
    out[...] = sent[0:32]


def place(rows, arrived, out, wide):
    def one(g, _):
        v = arrived[g] + arrived[16 + g]
        for c in range(4):
            r = pl.multiple_of(rows[0, g * 4 + c] * 4, 4)
            wide[pl.ds(r, 4), :] = v[c * 4 : c * 4 + 4]
        return 0

    lax.fori_loop(0, 16, one, 0)
    for i in range(8):
        for q in range(4):
            out[8 * i : 8 * i + 8, lanes(q)] = wide[pl.ds(32 * i + q, 8, stride=4), :]


FULL = pl.BlockSpec(memory_space=pltpu.VMEM)
SCALARS = pl.BlockSpec(memory_space=pltpu.SMEM)


def buf(*shape):
    return jax.ShapeDtypeStruct(shape, F32)


def call(kernel, n_scalars, n_arrays, outs, scratch=(), mib=8, us=2):
    return pl.pallas_call(
        kernel,
        in_specs=[SCALARS] * n_scalars + [FULL] * n_arrays,
        out_specs=[FULL] * len(outs),
        out_shape=list(outs),
        scratch_shapes=[pltpu.VMEM(shape, F32) for shape in scratch],
        compiler_params=pltpu.CompilerParams(vmem_limit_bytes=mib << 20),
        cost_estimate=pl.CostEstimate(
            flops=us * 1000000, bytes_accessed=us * 3000000, transcendentals=0
        ),
        name=kernel.__name__,
    )


RIM = (CX, 2 * W)


def call_pack_y():
    hbm = pl.BlockSpec(memory_space=pltpu.HBM)
    return pl.pallas_call(
        pack_y,
        in_specs=[hbm] * 3,
        out_specs=[FULL] * 4,
        out_shape=[buf(13, *RIM)] * 2 + [buf(12, *RIM)] * 2,
        scratch_shapes=[pltpu.VMEM((2, *RIM), F32), pltpu.SemaphoreType.DMA((2, 5))],
        compiler_params=pltpu.CompilerParams(vmem_limit_bytes=62 << 20),
        name="pack_y",
    )


def call_pack_x(count):
    return call(pack_x, 0, 3 + (count == 13), [buf(count * TE * 4, W)] * 2, us=1)


FIELD = (6, ROWS, W)
SENT = (32, 16, W)


def call_forward():
    ghosts = [(2, 13 * TE * 4, W), (2, 13, *RIM)]
    return call(
        forward, 2, 7, [buf(STEPS, *FIELD), buf(ROWS, W)], [FIELD, FIELD, *ghosts], 12, 15
    )


def call_adjoint():
    ghosts = [(2, 12 * TE * 4, W), (2, 12, *RIM)]
    return call(
        adjoint,
        2,
        8,
        [buf(*SENT)],
        [FIELD, FIELD, *ghosts, (2, ROWS, W), (LB * 8, W), (33, 16, W)],
        12,
        15,
    )


def per_device(
    forward_state,
    adjoint_state,
    permittivity,
    waveform,
    source_cell,
    block_owner,
    block_slot,
    owner_rows,
):
    rows_y = call_pack_y()(forward_state, adjoint_state, permittivity)
    fy_near, fy_far = swapped(*rows_y[:2], "gy")
    ay_near, ay_far = swapped(*rows_y[2:], "gy")
    own = [buf(6, TR * CX, W)] * 2
    forward_own = call(convert, 0, 2, [*own, buf(TR * CX, W)])(forward_state, permittivity)
    fy_near, fy_far, forward_own = lax.optimization_barrier((fy_near, fy_far, forward_own))
    fx_near, fx_far = swapped(
        *call_pack_x(13)(forward_state, permittivity, fy_far, fy_near), "gx"
    )
    ax_near, ax_far = swapped(*call_pack_x(12)(adjoint_state, ay_far, ay_near), "gx")
    adjoint_own = call(convert, 0, 1, own)(adjoint_state)
    fx_far, fx_near, adjoint_own = lax.optimization_barrier((fx_far, fx_near, adjoint_own))
    inc, factor = call_forward()(
        source_cell, waveform, *forward_own, fx_far, fx_near, fy_far, fy_near
    )
    ax_near, ax_far, inc = lax.optimization_barrier((ax_near, ax_far, inc))
    (outgoing,) = call_adjoint()(
        block_owner,
        block_slot,
        *adjoint_own,
        factor,
        inc,
        ax_far,
        ax_near,
        ay_far,
        ay_near,
    )
    arrived = lax.all_to_all(outgoing, ("src", "gy"), 0, 0, tiled=True)
    (placed,) = call(place, 1, 1, [buf(64, 512)], [(256, W)])(owner_rows, arrived)
    return placed


def solution(mesh):
    in_specs = (
        P("src", None, "gx", "gy"),
        P("src", None, "gx", "gy"),
        P("gx", "gy"),
        P("src", None),
        P("src", None),
        P("gx", "gy"),
        P("gx", "gy"),
        P(("gx", "gy"), None),
    )
    out_specs = P(("gx", "gy"), "src")
    return jax.shard_map(
        per_device, mesh=mesh, in_specs=in_specs, out_specs=out_specs, check_vma=False
    )
```
